256 devices in a mesh: wide: 64 (over z, x, core), narrow: 4 (over y).
Axes of the slice: x: 4, y: 4, z: 8, core: 2. Of those that a mesh axis runs over, the one named last changes fastest.
Arguments:
- snapshots: float32 [128, 4096, 1024], P('wide', None, 'narrow'), may hold values from -384 to 384
- snap_factor: float32 [128, 256], replicated, may hold values from 0 to 1
- row_factor: float32 [1024, 256], P('wide'), may hold values from 0 to 3
- col_factor: float32 [1024, 256], P('narrow'), may hold values from 0 to 3
- row_dual: float32 [1024, 256], P('wide'), may hold values from -0.5 to 0.5
- col_dual: float32 [1024, 256], P('narrow'), may hold values from -0.5 to 0.5
Outputs:
- row_new: float32 [1024, 256], P('wide')
- col_new: float32 [1024, 256], P('narrow')
- row_dual_new: float32 [1024, 256], P('wide')
- col_dual_new: float32 [1024, 256], P('narrow')
The draws below stay inside these ranges and needn't reach their ends.
All inputs are finite; a program needn't handle non-finite values.
Results may differ from the reference program's by a relative error of at most 0.00018.
Values sent between devices are 32-bit elements; how exact they have to be, the bound alone decides.
No kernel may reach another device: no remote copies, remote signals or barrier semaphores. Data moves between devices by JAX's collectives and lax.ppermute only.
A program may use at most 64 MiB of HBM per device.

```python
import jax
import jax.numpy as jnp
from jax import lax

ROWS = 4096
KEEP = 1024
COLS = 1024
RANK = 256
ADMM_STEPS = 3
SNAPS = 128


def factor_draw(key, count, width):
    several = jax.random.split(key, 3)
    entries = jax.random.uniform(several[0], (count, width), jnp.float32, 0.0, 1.0)
    position = jnp.arange(count, dtype=jnp.float32)[:, None] / count
    rising = jnp.power(3.0, position)
    row_scale = jnp.exp(jax.random.uniform(several[1], (count, 1), jnp.float32, -0.6931, 0.6931))
    col_scale = jnp.exp(jax.random.uniform(several[2], (1, width), jnp.float32, -0.6931, 0.6931))
    return jnp.clip(entries * rising * row_scale * col_scale / 4.0, 0.0, 3.0)


def draw_snap_factor(key, part):
    several = jax.random.split(jax.random.fold_in(key, 37), 2)
    entries = jax.random.uniform(several[0], (SNAPS, RANK), jnp.float32, 0.0, 1.0)
    groups = 8
    snap_group = lax_mod(jnp.arange(SNAPS, dtype=jnp.int32), groups)[:, None]
    column = jnp.arange(RANK, dtype=jnp.int32)
    col_group = jnp.zeros((RANK,), jnp.int32)
    for level in range(1, groups):
        col_group = col_group + (level * level * RANK <= groups * groups * column).astype(jnp.int32)
    weights = jnp.where(snap_group == col_group[None, :], 1.0, 0.05)
    col_scale = jnp.exp(jax.random.uniform(several[1], (1, RANK), jnp.float32, -1.386, 0.0))
    return jnp.clip(entries * weights * col_scale, 0.0, 1.0)


def lax_mod(values, divisor):
    return values % divisor


def draw_row_factor(key, part):
    return factor_draw(jax.random.fold_in(key, 11), KEEP, RANK)


def draw_col_factor(key, part):
    return factor_draw(jax.random.fold_in(key, 23), COLS, RANK)


def block_scale(own_key, shape, shards, smallest, high):
    gain = 1.0
    for axis_at, parts in shards:
        heights = jax.random.uniform(jax.random.fold_in(jax.random.fold_in(own_key, 6), axis_at), (parts,), jnp.float32, smallest / len(shards), high / len(shards))
        gain = gain * jnp.repeat(jnp.exp(heights), shape[axis_at] // parts).reshape((-1,) + (1,) * (len(shape) - 1 - axis_at))
    return gain


def scatter_about(rng, extent, deviation, limit, cuts=(), kind=jnp.bfloat16):
    values = jax.random.normal(rng, extent, jnp.float32) * deviation
    if len(cuts) > 0:
        values = block_scale(rng, extent, cuts, -0.22, 0.18) * values
    return jnp.clip(values, min=-limit, max=limit).astype(kind)


def setup_inputs(seed: int = 0) -> dict:
    splits = jax.random.split(jax.random.key(seed), 7)
    snapshots = scatter_about(splits[0], (SNAPS, ROWS, COLS), 64.0, 384.0, ((0, 64), (2, 4)), jnp.float32)
    snap_factor = draw_snap_factor(jax.random.fold_in(splits[6], 71), 0)
    row_factor = draw_row_factor(jax.random.fold_in(splits[6], 71), 0)
    col_factor = draw_col_factor(jax.random.fold_in(splits[6], 71), 0)
    row_dual = jnp.clip(jax.random.uniform(splits[4], (KEEP, RANK), jnp.float32, -0.5, 0.5) * block_scale(splits[4], (KEEP, RANK), ((0, 64),), -0.4, 0.0), -0.5, 0.5)
    col_dual = jnp.clip(jax.random.uniform(splits[5], (COLS, RANK), jnp.float32, -0.5, 0.5) * block_scale(splits[5], (COLS, RANK), ((0, 4),), -0.4, 0.0), -0.5, 0.5)
    return {"snapshots": snapshots, "snap_factor": snap_factor, "row_factor": row_factor, "col_factor": col_factor, "row_dual": row_dual, "col_dual": col_dual}


def dct_table():
    degree = lax.iota(jnp.int32, KEEP)[:, None]
    sample = lax.iota(jnp.int32, ROWS)[None, :]
    phases = (2 * sample + 1) * degree % (4 * ROWS)
    angles = phases.astype(jnp.float32) * (jnp.pi / (2 * ROWS))
    scales = jnp.where(degree == 0, (1.0 / ROWS) ** 0.5, (2.0 / ROWS) ** 0.5)
    return scales * jnp.cos(angles)

def admm_update(totals, gram_matrix, primal, multiplier):
    penalty = jnp.trace(gram_matrix) / gram_matrix.shape[0]
    system = gram_matrix + penalty * jnp.eye(gram_matrix.shape[0], dtype=gram_matrix.dtype)
    factor = jnp.linalg.cholesky(system)
    for repeat in range(ADMM_STEPS):
        target = totals + penalty * (primal + multiplier)
        solved = jax.scipy.linalg.cho_solve((factor, True), target.T).T
        primal = jnp.maximum(solved - multiplier, 0.0)
        multiplier = multiplier + primal - solved
    return (primal, multiplier)

def reference(snapshots, snap_factor, row_factor, col_factor, row_dual, col_dual):
    highest = lax.Precision.HIGHEST
    table = dct_table()
    compressed = jnp.einsum('kn,snj->skj', table, snapshots, precision=highest)
    flat = compressed.reshape(-1, compressed.shape[2])
    snap_gram = jnp.dot(snap_factor.T, snap_factor, precision=highest)
    row_gram = jnp.dot(row_factor.T, row_factor, precision=highest)
    khatri = (snap_factor[:, None, :] * row_factor[None, :, :]).reshape(-1, row_factor.shape[1])
    col_totals = jnp.dot(flat.T, khatri, precision=highest)
    col_new, col_dual_new = admm_update(col_totals, snap_gram * row_gram, col_factor, col_dual)
    col_gram = jnp.dot(col_new.T, col_new, precision=highest)
    projected = jnp.dot(flat, col_new, precision=highest).reshape(compressed.shape[0], compressed.shape[1], -1)
    row_totals = jnp.sum(projected * snap_factor[:, None, :], axis=0)
    row_new, row_dual_new = admm_update(row_totals, snap_gram * col_gram, row_factor, row_dual)
    return (row_new, col_new, row_dual_new, col_dual_new)
```

```python
import functools
import math

import jax
import jax.numpy as jnp
import numpy as np
from jax import lax
from jax.experimental import pallas as pl
from jax.experimental.pallas import tpu as pltpu
from jax.sharding import Mesh
from jax.sharding import PartitionSpec as P

ROWS = 4096
KEEP = 1024
RANK = 256
COLS = 256
ADMM_STEPS = 3
PART = ROWS // 4
BAND = KEEP // 4
STEP = 256
NZ, NX, NC, NY = 8, 4, 2, 4
WIDE = ("z", "x", "c")
F32 = jnp.float32
BF16 = jnp.bfloat16
VMEM = pl.BlockSpec(memory_space=pltpu.VMEM)
SMEM = pl.BlockSpec(memory_space=pltpu.SMEM)


def halves(table):
    high = table.astype(np.float32).astype(jnp.bfloat16)
    low = (table - high.astype(np.float64)).astype(np.float32).astype(jnp.bfloat16)
    return high, low


def twiddles():
    odd = 2 * np.arange(PART)[None, :] + 1
    degree = np.arange(BAND)[:, None]
    scale = math.sqrt(2.0 / ROWS)
    plain = scale * np.cos(np.pi * (odd * degree % 4096) / 2048)
    plain[0] = math.sqrt(1.0 / ROWS)
    angle = np.pi * (odd * (2 * degree + 1) % 8192) / 4096
    tables = []
    for table in (plain, scale * np.cos(angle), scale * np.sin(angle)):
        tables.extend(halves(table))
    turn = np.pi * odd.T / 8192
    lanes = np.ones((1, 128))
    return tables, (np.cos(turn) * lanes).astype(np.float32), (np.sin(turn) * lanes).astype(np.float32)


def split(value):
    high = value.astype(BF16)
    return high, (value - high.astype(F32)).astype(BF16)


def dot(a, b):
    return jnp.dot(a, b, preferred_element_type=F32)


def dot3(a, b):
    return dot(a[0], b[0]) + (dot(a[1], b[0]) + dot(a[0], b[1]))


def exact(a, b):
    return jnp.dot(a, b, precision=lax.Precision.HIGHEST, preferred_element_type=F32)


def turned(ref, s):
    index = 7 - lax.broadcasted_iota(jnp.int32, (8, COLS), 0)
    tiles = []
    for t in range(STEP // 8):
        tile = ref[s, STEP - 8 * (t + 1) : STEP - 8 * t, :]
        tiles.append(jnp.take_along_axis(tile, index, axis=0, mode="promise_in_bounds"))
    return jnp.concatenate(tiles, axis=0)


def dct_kernel(x0, x1, x2, x3, cos_ref, sin_ref, ah, al, bh, bl, ch, cl, out):
    @pl.when(pl.program_id(0) == 0)
    def _():
        out[...] = jnp.zeros_like(out)

    plain, even, odd = (ah[...], al[...]), (bh[...], bl[...]), (ch[...], cl[...])
    cos = jnp.concatenate([cos_ref[...]] * 2, axis=1)
    sin = jnp.concatenate([sin_ref[...]] * 2, axis=1)
    for s in range(2):
        first, third = x0[s], x2[s]
        second, fourth = turned(x1, s), turned(x3, s)
        outer, inner = first + fourth, second + third
        v, w = first - fourth, second - third
        out[s, 0] += dot3(plain, split(outer + inner))
        out[s, 2] += dot3(even, split(outer - inner))
        p = dot3(even, split(v * cos - w * sin))
        q = dot3(odd, split(v * sin + w * cos))
        out[s, 1] += p + q
        out[s, 3] += p - q


def dct(snapshots):
    tables, cos, sin = twiddles()
    steps = PART // STEP
    block = (2, STEP, COLS)
    table = pl.BlockSpec((BAND, STEP), lambda i: (0, i))
    turn = pl.BlockSpec((STEP, 128), lambda i: (i, 0))
    return pl.pallas_call(
        dct_kernel,
        grid=(steps,),
        in_specs=[
            pl.BlockSpec(block, lambda i: (0, i, 0)),
            pl.BlockSpec(block, lambda i: (0, 2 * steps - 1 - i, 0)),
            pl.BlockSpec(block, lambda i: (0, 2 * steps + i, 0)),
            pl.BlockSpec(block, lambda i: (0, 4 * steps - 1 - i, 0)),
            turn,
            turn,
        ]
        + [table] * 6,
        out_specs=pl.BlockSpec((2, 4, BAND, COLS), lambda i: (0, 0, 0, 0)),
        out_shape=jax.ShapeDtypeStruct((2, 4, BAND, COLS), F32),
        cost_estimate=pl.CostEstimate(flops=7_000_000_000, bytes_accessed=13_000_000, transcendentals=0),
        name="dct",
    )(*([snapshots] * 4), jnp.asarray(cos), jnp.asarray(sin), *map(jnp.asarray, tables))


def place_rows(where, pieces, rows):
    x, core = where[1], where[2]
    for side in range(NC):
        for shift in range(NX):
            source = lax.rem(x - shift + NX, NX)
            owner = core if side == 0 else 1 - core
            for z in range(NZ):
                start = pl.multiple_of(z * 128 + source * 32 + owner * 16, 16)
                block = pieces[side * NX + shift][z]
                for half in range(2):
                    rows[half, pl.ds(start, 16), :] = block[:, 128 * half : 128 * half + 128]


def totals_kernel(where, comp, snap, *refs):
    pieces, (keep, send), (rows, total) = refs[:8], refs[8:10], refs[10:]
    place_rows(where, pieces, rows)
    z, x, core = where[0], where[1], where[2]
    wide = (z * NX + x) * NC + core
    sums = [None, None]
    for k in range(4):
        line = [rows[half, pl.ds(k, BAND, stride=4), :] for half in range(2)]
        lines = split(jnp.concatenate(line, axis=1).T)
        for s in range(2):
            term = dot3(lines, split(comp[s, k]))
            sums[s] = term if sums[s] is None else sums[s] + term
    total[...] = sum(sums[s].T * snap[pl.ds(2 * wide + s, 1), :] for s in range(2))
    for shift in range(NX):
        target = lax.rem(x + shift, NX)
        for ref, owner in ((keep, core), (send, 1 - core)):
            start = pl.multiple_of(owner * 128 + target * 32, 32)
            ref[shift] = total[pl.ds(start, 32), :]


def totals(where, comp, snap, pieces):
    part = jax.ShapeDtypeStruct((NX, 32, RANK), F32)
    return pl.pallas_call(
        totals_kernel,
        in_specs=[SMEM] + [VMEM] * 10,
        out_specs=[VMEM] * 2,
        out_shape=[part] * 2,
        scratch_shapes=[pltpu.VMEM((2, KEEP, 128), F32), pltpu.VMEM((COLS, RANK), F32)],
        cost_estimate=pl.CostEstimate(flops=800_000_000, bytes_accessed=4_000_000, transcendentals=0),
        name="totals",
    )(where, comp, snap, *pieces)


def inverse(gram):
    eye = (
        lax.broadcasted_iota(jnp.int32, (RANK, RANK), 0)
        == lax.broadcasted_iota(jnp.int32, (RANK, RANK), 1)
    ).astype(F32)
    penalty = jnp.sum(gram * eye) / RANK
    system = gram / penalty + eye
    middle = 2.0 / (1.0 + 257.0)
    rest = eye - middle * system
    reach = 258.0 / 256.0
    found = middle * eye
    for step in range(6):
        doubled = 2.0 * reach * reach - 1.0
        gain = 2.0 * reach * reach / doubled
        if step == 0:
            found = (gain * middle) * (eye + rest)
        else:
            found = gain * (found + exact(found, rest))
        if step < 5:
            rest = gain * exact(rest, rest) - (1.0 / doubled) * eye
        reach = doubled
    found = found + exact(found, eye - exact(system, found))
    return found / penalty, penalty


def col_system_kernel(where, snap, *refs):
    pieces, (inv, pen), (rows,) = refs[:8], refs[8:10], refs[10:]
    place_rows(where, pieces, rows)
    snaps, lines = snap[...], jnp.concatenate([rows[0], rows[1]], axis=1)
    gram = exact(snaps.T, snaps) * exact(lines.T, lines)
    found, penalty = inverse(gram)
    inv[...] = found
    pen[...] = jnp.full((8, 128), penalty, F32)


def row_system_kernel(where, snap, mine, other, inv, pen, gram):
    core = where[2]
    gram[pl.ds(pl.multiple_of(core * 128, 128), 128), :] = mine[...]
    gram[pl.ds(pl.multiple_of((1 - core) * 128, 128), 128), :] = other[...]
    snaps = snap[...]
    found, penalty = inverse(exact(snaps.T, snaps) * gram[...])
    inv[...] = found
    pen[...] = jnp.full((8, 128), penalty, F32)


def system(kernel, where, snap, parts, scratch, name):
    return pl.pallas_call(
        kernel,
        in_specs=[SMEM] + [VMEM] * (1 + len(parts)),
        out_specs=[VMEM] * 2,
        out_shape=[
            jax.ShapeDtypeStruct((RANK, RANK), F32),
            jax.ShapeDtypeStruct((8, 128), F32),
        ],
        scratch_shapes=[scratch],
        cost_estimate=pl.CostEstimate(flops=3_000_000_000, bytes_accessed=1_000_000, transcendentals=0),
        name=name,
    )(where, snap, *parts)


def admm_update(sums, inv, penalty, primal, multiplier):
    for _ in range(ADMM_STEPS):
        solved = exact(sums + penalty * (primal + multiplier), inv)
        primal = jnp.maximum(solved - multiplier, 0.0)
        multiplier = multiplier + primal - solved
    return primal, multiplier


def col_kernel(where, comp, snap, inv, pen, factor, dual, *refs):
    pieces = refs[:8]
    new, dual_new, keep, send, gram_half = refs[8:13]
    total, mapped, gram = refs[13:]
    z, x, core = where[0], where[1], where[2]
    wide = (z * NX + x) * NC + core
    for side in range(NC):
        for shift in range(NX):
            source = lax.rem(x - shift + NX, NX)
            owner = core if side == 0 else 1 - core
            start = pl.multiple_of(owner * 128 + source * 32, 32)
            total[pl.ds(start, 32), :] = pieces[side * NX + shift][...]
    primal, multiplier = admm_update(total[...], inv[...], pen[0, 0], factor[...], dual[...])
    new[...] = primal
    dual_new[...] = multiplier
    gram[...] = exact(primal.T, primal)
    gram_half[...] = gram[pl.ds(pl.multiple_of(core * 128, 128), 128), :]
    weights = split(primal)
    for k in range(4):
        line = sum(
            dot3(split(comp[s, k]), weights) * snap[pl.ds(2 * wide + s, 1), :] for s in range(2)
        )
        for half in range(2):
            mapped[half, pl.ds(k, BAND, stride=4), :] = line[:, 128 * half : 128 * half + 128]
    for shift in range(NX):
        target = lax.rem(x + shift, NX)
        for ref, owner in ((keep, core), (send, 1 - core)):
            for line in range(NZ):
                start = pl.multiple_of(line * 128 + target * 32 + owner * 16, 16)
                for half in range(2):
                    ref[shift, line, :, 128 * half : 128 * half + 128] = mapped[half, pl.ds(start, 16), :]


def col_update(where, comp, snap, inv, pen, factor, dual, pieces):
    square = jax.ShapeDtypeStruct((COLS, RANK), F32)
    part = jax.ShapeDtypeStruct((NX, NZ, 16, RANK), F32)
    return pl.pallas_call(
        col_kernel,
        in_specs=[SMEM] + [VMEM] * 3 + [VMEM] * 11,
        out_specs=[VMEM] * 5,
        out_shape=[square, square, part, part, jax.ShapeDtypeStruct((128, RANK), F32)],
        scratch_shapes=[
            pltpu.VMEM((COLS, RANK), F32),
            pltpu.VMEM((2, KEEP, 128), F32),
            pltpu.VMEM((RANK, RANK), F32),
        ],
        cost_estimate=pl.CostEstimate(flops=1_500_000_000, bytes_accessed=5_000_000, transcendentals=0),
        name="col_update",
    )(where, comp, snap, inv, pen, factor, dual, *pieces)


def in_order(where, parts, held):
    y = where[3]
    for shift in range(NY):
        held[lax.rem(y - shift + NY, NY)] = parts[shift][...]
    return (held[0] + held[1]) + (held[2] + held[3])


def sum_kernel(where, *refs):
    parts, out, held = refs[:4], refs[4], refs[5]
    out[...] = in_order(where, parts, held)


def ordered_sum(where, parts):
    shape = parts[0].shape
    return pl.pallas_call(
        sum_kernel,
        in_specs=[SMEM] + [VMEM] * 4,
        out_specs=VMEM,
        out_shape=jax.ShapeDtypeStruct(shape, F32),
        scratch_shapes=[pltpu.VMEM((NY, *shape), F32)],
        name="ordered_sum",
    )(where, *parts)


def row_kernel(where, inv, pen, factor, dual, *refs):
    parts, (new, dual_new), held = refs[:4], refs[4:6], refs[6]
    sums = in_order(where, parts, held)
    primal, multiplier = admm_update(sums, inv[...], pen[0, 0], factor[...], dual[...])
    new[...] = primal
    dual_new[...] = multiplier


def row_update(where, inv, pen, factor, dual, parts):
    own = jax.ShapeDtypeStruct((16, RANK), F32)
    return pl.pallas_call(
        row_kernel,
        in_specs=[SMEM] + [VMEM] * 8,
        out_specs=[VMEM] * 2,
        out_shape=[own] * 2,
        scratch_shapes=[pltpu.VMEM((NY, 16, RANK), F32)],
        name="row_update",
    )(where, inv, pen, factor, dual, *parts)


def shifted(array, axis, size, by):
    return lax.ppermute(array, axis, [(i, (i + by) % size) for i in range(size)])


def from_all(array, axis, size):
    return [array] + [shifted(array, axis, size, by) for by in range(1, size)]


def copied_along_z(array):
    whole = jnp.broadcast_to(array[None], (NZ, *array.shape))
    return lax.all_to_all(whole, "z", 0, 0, tiled=True)


def body(snapshots, snap_factor, row_factor, col_factor, row_dual, col_dual):
    where = jnp.stack([lax.axis_index(name) for name in ("z", "x", "c", "y")]).astype(jnp.int32)
    lines = from_all(copied_along_z(row_factor), "x", NX)
    lines = lines + [shifted(line, "c", NC, 1) for line in lines]
    comp = dct(snapshots)
    keep, send = totals(where, comp, snap_factor, lines)
    inv, pen = system(
        col_system_kernel, where, snap_factor, lines, pltpu.VMEM((2, KEEP, 128), F32), "col_system"
    )
    half = keep + shifted(send, "c", NC, 1)
    chunk = half[0] + sum(shifted(half[by], "x", NX, by) for by in range(1, NX))
    chunk = copied_along_z(chunk).sum(axis=0)
    pieces = from_all(chunk, "x", NX)
    pieces = pieces + [shifted(piece, "c", NC, 1) for piece in pieces]
    col_new, col_dual_new, keep, send, gram_half = col_update(
        where, comp, snap_factor, inv, pen, col_factor, col_dual, pieces
    )
    gram_mine = ordered_sum(where, from_all(gram_half, "y", NY))
    gram_other = shifted(gram_mine, "c", NC, 1)
    inv, pen = system(
        row_system_kernel, where, snap_factor, [gram_mine, gram_other], pltpu.VMEM((RANK, RANK), F32), "row_system"
    )
    half = keep + shifted(send, "c", NC, 1)
    block = half[0] + sum(shifted(half[by], "x", NX, by) for by in range(1, NX))
    mine = lax.all_to_all(block, "z", 0, 0, tiled=True).sum(axis=0)
    row_new, row_dual_new = row_update(
        where, inv, pen, row_factor, row_dual, from_all(mine, "y", NY)
    )
    return row_new, col_new, row_dual_new, col_dual_new


def solution(mesh):
    fine = Mesh(mesh.devices.reshape(NZ, NX, NC, NY), ("z", "x", "c", "y"))
    return jax.shard_map(
        body,
        mesh=fine,
        in_specs=(
            P(WIDE, None, "y"),
            P(),
            P(WIDE, None),
            P("y", None),
            P(WIDE, None),
            P("y", None),
        ),
        out_specs=(P(WIDE, None), P("y", None), P(WIDE, None), P("y", None)),
        check_vma=False,
    )
```

```python
import math

import jax
import jax.numpy as jnp
import numpy as np
from jax import lax
from jax.experimental import pallas as pl
from jax.experimental.pallas import tpu as pltpu
from jax.sharding import Mesh
from jax.sharding import PartitionSpec as P

ROWS = 4096
KEEP = 1024
RANK = 256
COLS = 256
ADMM_STEPS = 3
PART = ROWS // 4
BAND = KEEP // 4
STEP = 256
NZ, NX, NC, NY = 8, 4, 2, 4
WIDE = ("z", "x", "c")
F32 = jnp.float32
BF16 = jnp.bfloat16
VMEM = pl.BlockSpec(memory_space=pltpu.VMEM)


def twiddles():
    odd = 2 * np.arange(STEP)[None, :] + 1
    degree = np.arange(BAND)[:, None]
    scale = math.sqrt(2.0 / ROWS)
    angles = np.pi * odd * degree / 2048, np.pi * odd * (2 * degree + 1) / 4096
    weight = np.where(degree == 0, math.sqrt(1.0 / ROWS), scale), scale
    base = [w * f(a) for w, a in zip(weight, angles) for f in (np.cos, np.sin)]
    lanes = np.ones((1, 128))
    eight = np.arange(8)[:, None] * lanes
    ahead = [f(a) for a in (np.pi * eight / 4, np.pi * (2 * eight + 1) / 8) for f in (np.cos, np.sin)]
    turn = np.pi * (2 * eight + 1) / 8192
    tables = base + [np.stack(ahead + [np.cos(turn), np.sin(turn)])]
    return [jnp.asarray(table.astype(np.float32)) for table in tables]


def room(mebibytes):
    return pltpu.CompilerParams(vmem_limit_bytes=mebibytes * 2**20)


def split(value):
    high = value.astype(BF16)
    return high, (value - high.astype(F32)).astype(BF16)


def dot(a, b):
    return jnp.dot(a, b, preferred_element_type=F32)


def dot3(a, b):
    return dot(a[0], b[0]) + (dot(a[1], b[0]) + dot(a[0], b[1]))


def exact(a, b):
    return jnp.dot(a, b, precision=lax.Precision.HIGHEST, preferred_element_type=F32)


def twice(value):
    return jnp.concatenate([value, value], axis=1)


def turned(ref, s):
    index = 7 - lax.broadcasted_iota(jnp.int32, (8, COLS), 0)
    tiles = []
    for t in range(STEP // 8):
        tile = ref[s, STEP - 8 * (t + 1) : STEP - 8 * t, :]
        tiles.append(jnp.take_along_axis(tile, index, axis=0, mode="promise_in_bounds"))
    return jnp.concatenate(tiles, axis=0)


def dct_kernel(x0, x1, x2, x3, *refs):
    base, ahead, outs = refs[:4], refs[4], refs[5:9]
    held, rotated, total = refs[9:13], refs[13:15], refs[15]
    high, low, high_t, low_t = outs
    step = pl.program_id(0)

    @pl.when(step == 0)
    def _():
        total[...] = jnp.zeros_like(total)
        for ref, first in zip(held, base):
            ref[...] = first[...]
        cos, sin = ahead[4], ahead[5]
        for t in range(STEP // 8):
            by_cos, by_sin = math.cos(math.pi * t / 512), math.sin(math.pi * t / 512)
            rotated[0][8 * t : 8 * t + 8, :] = cos * by_cos - sin * by_sin
            rotated[1][8 * t : 8 * t + 8, :] = sin * by_cos + cos * by_sin

    @pl.when(step > 0)
    def _():
        for pair in range(2):
            cos, sin = held[2 * pair][...], held[2 * pair + 1][...]
            by_cos = jnp.concatenate([twice(ahead[2 * pair])] * 32, axis=0)
            by_sin = jnp.concatenate([twice(ahead[2 * pair + 1])] * 32, axis=0)
            held[2 * pair][...] = cos * by_cos - sin * by_sin
            held[2 * pair + 1][...] = sin * by_cos + cos * by_sin
        cos, sin = rotated[0][...], rotated[1][...]
        by_cos, by_sin = math.cos(math.pi / 16), math.sin(math.pi / 16)
        rotated[0][...] = cos * by_cos - sin * by_sin
        rotated[1][...] = sin * by_cos + cos * by_sin

    plain, even, odd = split(held[0][...]), split(held[2][...]), split(held[3][...])
    cos, sin = twice(rotated[0][...]), twice(rotated[1][...])
    for s in range(2):
        first, third = x0[s], x2[s]
        second, fourth = turned(x1, s), turned(x3, s)
        outer, inner = first + fourth, second + third
        v, w = first - fourth, second - third
        total[s, 0] += dot3(plain, split(outer + inner))
        total[s, 2] += dot3(even, split(outer - inner))
        p = dot3(even, split(v * cos - w * sin))
        q = dot3(odd, split(v * sin + w * cos))
        total[s, 1] += p + q
        total[s, 3] += p - q

    @pl.when(step == pl.num_programs(0) - 1)
    def _():
        for s in range(2):
            for k in range(4):
                high[s, k], low[s, k] = split(total[s, k])
                place = slice(BAND * k, BAND * (k + 1))
                high_t[s, :, place], low_t[s, :, place] = split(total[s, k].T)


def dct(snapshots):
    tables = twiddles()
    steps = PART // STEP
    block = (2, STEP, COLS)
    square = pltpu.VMEM((BAND, STEP), F32)
    turn = pltpu.VMEM((STEP, 128), F32)
    straight = jax.ShapeDtypeStruct((2, 4, BAND, COLS), BF16)
    crossed = jax.ShapeDtypeStruct((2, COLS, KEEP), BF16)

    def whole(shape):
        return pl.BlockSpec(shape, lambda i: (0,) * len(shape))

    return pl.pallas_call(
        dct_kernel,
        grid=(steps,),
        in_specs=[
            pl.BlockSpec(block, lambda i: (0, i, 0)),
            pl.BlockSpec(block, lambda i: (0, 2 * steps - 1 - i, 0)),
            pl.BlockSpec(block, lambda i: (0, 2 * steps + i, 0)),
            pl.BlockSpec(block, lambda i: (0, 4 * steps - 1 - i, 0)),
        ]
        + [whole(table.shape) for table in tables],
        out_specs=[whole(a.shape) for a in (straight, straight, crossed, crossed)],
        out_shape=[straight, straight, crossed, crossed],
        scratch_shapes=[square] * 4 + [turn] * 2 + [pltpu.VMEM((2, 4, BAND, COLS), F32)],
        cost_estimate=pl.CostEstimate(flops=7_000_000_000, bytes_accessed=13_000_000, transcendentals=0),
        compiler_params=room(24),
        name="dct",
    )(*([snapshots] * 4), *tables)


def place_of_own():
    return tuple(lax.axis_index(name) for name in ("z", "x", "c", "y"))


def own_weights(snap, z, x, core):
    wide = (z * NX + x) * NC + core
    return [snap[pl.ds(2 * wide + s, 1), :] for s in range(2)]


def place_rows(core, mine, other, rows):
    for ref, owner in ((mine, core), (other, 1 - core)):
        for group in range(NZ * NX):
            start = pl.multiple_of(group * 32 + owner * 16, 16)
            for half in range(2):
                rows[half, pl.ds(start, 16), :] = ref[group, :, 128 * half : 128 * half + 128]


def totals_kernel(high_t, low_t, snap, mine, other, keep, send, rows, total):
    z, x, core, _ = place_of_own()
    place_rows(core, mine, other, rows)
    sums = [0.0, 0.0]
    for k in range(4):
        line = [rows[half, pl.ds(k, BAND, stride=4), :] for half in range(2)]
        lines = split(jnp.concatenate(line, axis=1))
        place = slice(BAND * k, BAND * (k + 1))
        for s in range(2):
            sums[s] += dot3((high_t[s, :, place], low_t[s, :, place]), lines)
    weights = own_weights(snap, z, x, core)
    total[...] = sums[0] * weights[0] + sums[1] * weights[1]
    for shift in range(NX):
        target = lax.rem(x + shift, NX)
        for ref, owner in ((keep, core), (send, 1 - core)):
            start = pl.multiple_of(owner * 128 + target * 32, 32)
            ref[shift] = total[pl.ds(start, 32), :]


def totals(high_t, low_t, snap, mine, other):
    part = jax.ShapeDtypeStruct((NX, 32, RANK), F32)
    return pl.pallas_call(
        totals_kernel,
        in_specs=[VMEM] * 5,
        out_specs=[VMEM] * 2,
        out_shape=[part] * 2,
        scratch_shapes=[pltpu.VMEM((2, KEEP, 128), F32), pltpu.VMEM((COLS, RANK), F32)],
        cost_estimate=pl.CostEstimate(flops=800_000_000, bytes_accessed=4_000_000, transcendentals=0),
        compiler_params=room(12),
        name="totals",
    )(high_t, low_t, snap, mine, other)


def inverse(gram, state):
    eye = (
        lax.broadcasted_iota(jnp.int32, (RANK, RANK), 0)
        == lax.broadcasted_iota(jnp.int32, (RANK, RANK), 1)
    ).astype(F32)
    penalty = jnp.sum(gram * eye) / RANK
    system = gram / penalty + eye
    middle = 2.0 / (1.0 + 257.0)
    state[:RANK] = middle * eye
    state[RANK:] = eye - middle * system

    def double(step, reach):
        doubled = 2.0 * reach * reach - 1.0
        gain = 2.0 * reach * reach / doubled
        both = state[...]
        product = gain * dot3(split(both), split(both[RANK:]))
        state[:RANK] = gain * both[:RANK] + product[:RANK]
        state[RANK:] = product[RANK:] - (1.0 / doubled) * eye
        return doubled

    lax.fori_loop(0, 6, double, jnp.float32(258.0 / 256.0))
    found = state[:RANK]
    found = found + dot3(split(found), split(eye - exact(system, found)))
    return found / penalty, penalty


def col_system_kernel(snap, mine, other, inv, pen, rows, state):
    _, _, core, _ = place_of_own()
    place_rows(core, mine, other, rows)
    snaps, lines = snap[...], jnp.concatenate([rows[0], rows[1]], axis=1)
    found, penalty = inverse(exact(snaps.T, snaps) * exact(lines.T, lines), state)
    inv[...] = found
    pen[...] = jnp.full((8, 128), penalty, F32)


def row_system_kernel(snap, mine, other, inv, pen, gram, state):
    _, _, core, _ = place_of_own()
    gram[pl.ds(pl.multiple_of(core * 128, 128), 128), :] = mine[...]
    gram[pl.ds(pl.multiple_of((1 - core) * 128, 128), 128), :] = other[...]
    snaps = snap[...]
    found, penalty = inverse(exact(snaps.T, snaps) * gram[...], state)
    inv[...] = found
    pen[...] = jnp.full((8, 128), penalty, F32)


def system(kernel, snap, mine, other, scratch, name):
    return pl.pallas_call(
        kernel,
        in_specs=[VMEM] * 3,
        out_specs=[VMEM] * 2,
        out_shape=[
            jax.ShapeDtypeStruct((RANK, RANK), F32),
            jax.ShapeDtypeStruct((8, 128), F32),
        ],
        scratch_shapes=[pltpu.VMEM(scratch, F32), pltpu.VMEM((2 * RANK, RANK), F32)],
        cost_estimate=pl.CostEstimate(flops=3_000_000_000, bytes_accessed=1_000_000, transcendentals=0),
        compiler_params=room(8),
        name=name,
    )(snap, mine, other)


def admm_update(sums, inv, penalty, factor, dual, new, dual_new):
    new[...] = factor[...]
    dual_new[...] = dual[...]

    def update(step, carry):
        primal, multiplier = new[...], dual_new[...]
        solved = exact(sums[...] + penalty * (primal + multiplier), inv[...])
        primal = jnp.maximum(solved - multiplier, 0.0)
        new[...] = primal
        dual_new[...] = multiplier + primal - solved
        return carry

    lax.fori_loop(0, ADMM_STEPS, update, 0)


def col_kernel(high, low, snap, inv, pen, factor, dual, *refs):
    pieces = refs[:8]
    new, dual_new, keep, send, gram_half = refs[8:13]
    total, mapped, gram = refs[13:]
    z, x, core, _ = place_of_own()
    for side in range(NC):
        for shift in range(NX):
            source = lax.rem(x - shift + NX, NX)
            owner = core if side == 0 else 1 - core
            start = pl.multiple_of(owner * 128 + source * 32, 32)
            total[pl.ds(start, 32), :] = pieces[side * NX + shift][...]
    admm_update(total, inv, pen[0, 0], factor, dual, new, dual_new)
    primal = new[...]
    gram[...] = exact(primal.T, primal)
    gram_half[...] = gram[pl.ds(pl.multiple_of(core * 128, 128), 128), :]
    lines, weights = split(primal), own_weights(snap, z, x, core)
    for k in range(4):
        line = sum(dot3((high[s, k], low[s, k]), lines) * weights[s] for s in range(2))
        for half in range(2):
            mapped[half, pl.ds(k, BAND, stride=4), :] = line[:, 128 * half : 128 * half + 128]
    for shift in range(NX):
        target = lax.rem(x + shift, NX)
        for ref, owner in ((keep, core), (send, 1 - core)):
            for line in range(NZ):
                start = pl.multiple_of(line * 128 + target * 32 + owner * 16, 16)
                for half in range(2):
                    ref[shift, line, :, 128 * half : 128 * half + 128] = mapped[half, pl.ds(start, 16), :]


def col_update(high, low, snap, inv, pen, factor, dual, pieces):
    square = jax.ShapeDtypeStruct((COLS, RANK), F32)
    part = jax.ShapeDtypeStruct((NX, NZ, 16, RANK), F32)
    return pl.pallas_call(
        col_kernel,
        in_specs=[VMEM] * 15,
        out_specs=[VMEM] * 5,
        out_shape=[square, square, part, part, jax.ShapeDtypeStruct((128, RANK), F32)],
        scratch_shapes=[
            pltpu.VMEM((COLS, RANK), F32),
            pltpu.VMEM((2, KEEP, 128), F32),
            pltpu.VMEM((RANK, RANK), F32),
        ],
        cost_estimate=pl.CostEstimate(flops=1_500_000_000, bytes_accessed=5_000_000, transcendentals=0),
        compiler_params=room(14),
        name="col_update",
    )(high, low, snap, inv, pen, factor, dual, *pieces)


def in_order(parts, held):
    y = lax.axis_index("y")
    for shift in range(NY):
        held[lax.rem(y - shift + NY, NY)] = parts[shift][...]
    return (held[0] + held[1]) + (held[2] + held[3])


def sum_kernel(*refs):
    parts, out, held = refs[:4], refs[4], refs[5]
    out[...] = in_order(parts, held)


def ordered_sum(parts):
    shape = parts[0].shape
    return pl.pallas_call(
        sum_kernel,
        in_specs=[VMEM] * 4,
        out_specs=VMEM,
        out_shape=jax.ShapeDtypeStruct(shape, F32),
        scratch_shapes=[pltpu.VMEM((NY, *shape), F32)],
        compiler_params=room(4),
        name="ordered_sum",
    )(*parts)


def row_kernel(inv, pen, factor, dual, *refs):
    parts, (new, dual_new), held = refs[:4], refs[4:6], refs[6]
    held[0] = in_order(parts, held)
    admm_update(held.at[0], inv, pen[0, 0], factor, dual, new, dual_new)


def row_update(inv, pen, factor, dual, parts):
    own = jax.ShapeDtypeStruct((16, RANK), F32)
    return pl.pallas_call(
        row_kernel,
        in_specs=[VMEM] * 8,
        out_specs=[VMEM] * 2,
        out_shape=[own] * 2,
        scratch_shapes=[pltpu.VMEM((NY, 16, RANK), F32)],
        compiler_params=room(4),
        name="row_update",
    )(inv, pen, factor, dual, *parts)


def shifted(array, axis, size, by):
    return lax.ppermute(array, axis, [(i, (i + by) % size) for i in range(size)])


def from_all(array, axis, size):
    return [array] + [shifted(array, axis, size, by) for by in range(1, size)]


def copied_along(array, axes, size):
    whole = jnp.broadcast_to(array[None], (size, *array.shape))
    return lax.all_to_all(whole, axes, 0, 0, tiled=True)


def body(snapshots, snap_factor, row_factor, col_factor, row_dual, col_dual):
    mine = copied_along(row_factor, ("z", "x"), NZ * NX)
    high, low, high_t, low_t = dct(snapshots)
    mine, high_t = lax.optimization_barrier((mine, high_t))
    other = shifted(mine, "c", NC, 1)
    keep, send = totals(high_t, low_t, snap_factor, mine, other)
    inv, pen = system(
        col_system_kernel, snap_factor, mine, other, (2, KEEP, 128), "col_system"
    )
    half = keep + shifted(send, "c", NC, 1)
    chunk = half[0] + sum(shifted(half[by], "x", NX, by) for by in range(1, NX))
    chunk = copied_along(chunk, "z", NZ)
    chunk, inv = lax.optimization_barrier((chunk, inv))
    pieces = from_all(chunk.sum(axis=0), "x", NX)
    pieces = pieces + [shifted(piece, "c", NC, 1) for piece in pieces]
    col_new, col_dual_new, keep, send, gram_half = col_update(
        high, low, snap_factor, inv, pen, col_factor, col_dual, pieces
    )
    gram_mine = ordered_sum(from_all(gram_half, "y", NY))
    gram_other = shifted(gram_mine, "c", NC, 1)
    inv, pen = system(
        row_system_kernel, snap_factor, gram_mine, gram_other, (RANK, RANK), "row_system"
    )
    half = keep + shifted(send, "c", NC, 1)
    block = half[0] + sum(shifted(half[by], "x", NX, by) for by in range(1, NX))
    block = lax.all_to_all(block, "z", 0, 0, tiled=True)
    block, inv = lax.optimization_barrier((block, inv))
    row_new, row_dual_new = row_update(
        inv, pen, row_factor, row_dual, from_all(block.sum(axis=0), "y", NY)
    )
    return row_new, col_new, row_dual_new, col_dual_new


def solution(mesh):
    fine = Mesh(mesh.devices.reshape(NZ, NX, NC, NY), ("z", "x", "c", "y"))
    return jax.shard_map(
        body,
        mesh=fine,
        in_specs=(
            P(WIDE, None, "y"),
            P(),
            P(WIDE, None),
            P("y", None),
            P(WIDE, None),
            P("y", None),
        ),
        out_specs=(P(WIDE, None), P("y", None), P(WIDE, None), P("y", None)),
        check_vma=False,
    )
```

```python
import functools
import math

import jax
import jax.numpy as jnp
import numpy as np
from jax import lax
from jax.experimental import pallas as pl
from jax.experimental.pallas import tpu as pltpu
from jax.sharding import Mesh
from jax.sharding import PartitionSpec as P


ROWS = 4096
KEEP = 1024
RANK = 256
COLS = 256
ADMM_STEPS = 3
PART = ROWS // 4
BAND = KEEP // 4
STEP = 256
NZ, NX, NC, NY = 8, 4, 2, 4
WIDE = ("z", "x", "c")
F32 = jnp.float32
BF16 = jnp.bfloat16
VMEM = pl.BlockSpec(memory_space=pltpu.VMEM)


def twiddles():
    odd = 2 * np.arange(STEP)[None, :] + 1
    degree = np.arange(BAND)[:, None]
    scale = math.sqrt(2.0 / ROWS)
    angles = np.pi * odd * degree / 2048, np.pi * odd * (2 * degree + 1) / 4096
    weight = np.where(degree == 0, math.sqrt(1.0 / ROWS), scale), scale
    base = [w * f(a) for w, a in zip(weight, angles) for f in (np.cos, np.sin)]
    lanes = np.ones((1, 128))
    eight = np.arange(8)[:, None] * lanes
    ahead = [f(a) for a in (np.pi * eight / 4, np.pi * (2 * eight + 1) / 8) for f in (np.cos, np.sin)]
    turn = np.pi * (2 * eight + 1) / 8192
    tables = np.stack(base), np.stack(ahead + [np.cos(turn), np.sin(turn)])
    return [jnp.asarray(table.astype(np.float32)) for table in tables]


def room(mebibytes):
    return pltpu.CompilerParams(vmem_limit_bytes=mebibytes * 2**20)


def split(value):
    high = value.astype(BF16)
    return high, (value - high.astype(F32)).astype(BF16)


def dot(a, b):
    return jnp.dot(a, b, preferred_element_type=F32)


def dot3(a, b):
    return dot(a[0], b[0]) + (dot(a[1], b[0]) + dot(a[0], b[1]))


def exact(a, b):
    return jnp.dot(a, b, precision=lax.Precision.HIGHEST, preferred_element_type=F32)


def twice(value):
    return jnp.concatenate([value, value], axis=1)


def turned(ref, s):
    index = 7 - lax.broadcasted_iota(jnp.int32, (8, COLS), 0)
    tiles = []
    for t in range(STEP // 8):
        tile = ref[s, STEP - 8 * (t + 1) : STEP - 8 * t, :]
        tiles.append(jnp.take_along_axis(tile, index, axis=0, mode="promise_in_bounds"))
    return jnp.concatenate(tiles, axis=0)


def dct_kernel(x0, x1, x2, x3, *refs):
    base, ahead, outs = refs[0], refs[1], refs[2:6]
    held, rotated, total = refs[6], refs[7:9], refs[9]
    high, low, high_t, low_t = outs
    step = pl.program_id(0)

    @pl.when(step == 0)
    def _():
        total[...] = jnp.zeros_like(total)
        held[...] = base[...]
        cos, sin = ahead[4], ahead[5]
        for t in range(STEP // 8):
            by_cos, by_sin = math.cos(math.pi * t / 512), math.sin(math.pi * t / 512)
            rotated[0][8 * t : 8 * t + 8, :] = cos * by_cos - sin * by_sin
            rotated[1][8 * t : 8 * t + 8, :] = sin * by_cos + cos * by_sin

    @pl.when(step > 0)
    def _():
        for pair in range(2):
            cos, sin = held[2 * pair], held[2 * pair + 1]
            by_cos = jnp.concatenate([twice(ahead[2 * pair])] * 32, axis=0)
            by_sin = jnp.concatenate([twice(ahead[2 * pair + 1])] * 32, axis=0)
            held[2 * pair] = cos * by_cos - sin * by_sin
            held[2 * pair + 1] = sin * by_cos + cos * by_sin
        cos, sin = rotated[0][...], rotated[1][...]
        by_cos, by_sin = math.cos(math.pi / 16), math.sin(math.pi / 16)
        rotated[0][...] = cos * by_cos - sin * by_sin
        rotated[1][...] = sin * by_cos + cos * by_sin

    plain, even, odd = split(held[0]), split(held[2]), split(held[3])
    cos, sin = twice(rotated[0][...]), twice(rotated[1][...])
    for s in range(2):
        first, third = x0[s], x2[s]
        second, fourth = turned(x1, s), turned(x3, s)
        outer, inner = first + fourth, second + third
        v, w = first - fourth, second - third
        total[s, 0] += dot3(plain, split(outer + inner))
        total[s, 2] += dot3(even, split(outer - inner))
        p = dot3(even, split(v * cos - w * sin))
        q = dot3(odd, split(v * sin + w * cos))
        total[s, 1] += p + q
        total[s, 3] += p - q

    @pl.when(step == pl.num_programs(0) - 1)
    def _():
        for s in range(2):
            for k in range(4):
                high[s, k], low[s, k] = split(total[s, k])
                place = slice(BAND * k, BAND * (k + 1))
                high_t[s, :, place], low_t[s, :, place] = split(total[s, k].T)


def dct(snapshots):
    tables = twiddles()
    steps = PART // STEP
    block = (2, STEP, COLS)
    turn = pltpu.VMEM((STEP, 128), F32)
    straight = jax.ShapeDtypeStruct((2, 4, BAND, COLS), BF16)
    crossed = jax.ShapeDtypeStruct((2, COLS, KEEP), BF16)

    def whole(shape):
        return pl.BlockSpec(shape, lambda i: (0,) * len(shape))

    return pl.pallas_call(
        dct_kernel,
        grid=(steps,),
        in_specs=[
            pl.BlockSpec(block, lambda i: (0, i, 0)),
            pl.BlockSpec(block, lambda i: (0, 2 * steps - 1 - i, 0)),
            pl.BlockSpec(block, lambda i: (0, 2 * steps + i, 0)),
            pl.BlockSpec(block, lambda i: (0, 4 * steps - 1 - i, 0)),
        ]
        + [whole(table.shape) for table in tables],
        out_specs=[whole(a.shape) for a in (straight, straight, crossed, crossed)],
        out_shape=[straight, straight, crossed, crossed],
        scratch_shapes=[
            pltpu.VMEM((4, BAND, STEP), F32),
            turn,
            turn,
            pltpu.VMEM((2, 4, BAND, COLS), F32),
        ],
        cost_estimate=pl.CostEstimate(flops=7_000_000_000, bytes_accessed=13_000_000, transcendentals=0),
        compiler_params=room(46),
        name="dct",
    )(*([snapshots] * 4), *tables)


def place_of_own():
    return tuple(lax.axis_index(name) for name in ("z", "x", "c", "y"))


FLIPS = (0, 3, 1, 2)


def flipped(position, flip):
    high, low = position // 2, position % 2
    high = 1 - high if flip // 2 else high
    low = 1 - low if flip % 2 else low
    return 2 * high + low


def own_weights(snap, z, x, core):
    wide = (z * NX + x) * NC + core
    return [snap[pl.ds(2 * wide + s, 1), :] for s in range(2)]


def place_rows(core, mine, other, rows):
    for ref, owner in ((mine, core), (other, 1 - core)):
        for group in range(NZ * NX):
            start = pl.multiple_of(group * 32 + owner * 16, 16)
            for half in range(2):
                rows[half, pl.ds(start, 16), :] = ref[group, :, 128 * half : 128 * half + 128]


def totals_kernel(high_t, low_t, snap, mine, other, keep, send, rows, total):
    z, x, core, _ = place_of_own()
    place_rows(core, mine, other, rows)
    sums = [0.0, 0.0]
    for k in range(4):
        line = [rows[half, pl.ds(k, BAND, stride=4), :] for half in range(2)]
        lines = split(jnp.concatenate(line, axis=1))
        place = slice(BAND * k, BAND * (k + 1))
        for s in range(2):
            sums[s] += dot3((high_t[s, :, place], low_t[s, :, place]), lines)
    weights = own_weights(snap, z, x, core)
    total[...] = sums[0] * weights[0] + sums[1] * weights[1]
    for at, flip in enumerate(FLIPS):
        for ref, owner in ((keep, core), (send, 1 - core)):
            start = pl.multiple_of(owner * 128 + flipped(x, flip) * 32, 32)
            ref[at] = total[pl.ds(start, 32), :]


def totals(high_t, low_t, snap, mine, other):
    part = jax.ShapeDtypeStruct((NX, 32, RANK), F32)
    return pl.pallas_call(
        totals_kernel,
        in_specs=[VMEM] * 5,
        out_specs=[VMEM] * 2,
        out_shape=[part] * 2,
        scratch_shapes=[pltpu.VMEM((2, KEEP, 128), F32), pltpu.VMEM((COLS, RANK), F32)],
        cost_estimate=pl.CostEstimate(flops=800_000_000, bytes_accessed=4_000_000, transcendentals=0),
        compiler_params=room(12),
        name="totals",
    )(high_t, low_t, snap, mine, other)


def inverse(gram, state):
    eye = (
        lax.broadcasted_iota(jnp.int32, (RANK, RANK), 0)
        == lax.broadcasted_iota(jnp.int32, (RANK, RANK), 1)
    ).astype(F32)
    penalty = jnp.sum(gram * eye) / RANK
    system = gram / penalty + eye
    middle = 2.0 / (1.0 + 257.0)
    state[:RANK] = middle * eye
    state[RANK:] = eye - middle * system

    def double(step, reach):
        doubled = 2.0 * reach * reach - 1.0
        gain = 2.0 * reach * reach / doubled
        both = state[...]
        product = gain * dot3(split(both), split(both[RANK:]))
        state[:RANK] = gain * both[:RANK] + product[:RANK]
        state[RANK:] = product[RANK:] - (1.0 / doubled) * eye
        return doubled

    lax.fori_loop(0, 6, double, jnp.float32(258.0 / 256.0))
    found = state[:RANK]
    found = found + dot3(split(found), split(eye - exact(system, found)))
    return found / penalty, penalty


def col_system_kernel(snap, mine, other, inv, pen, rows, state):
    _, _, core, _ = place_of_own()
    place_rows(core, mine, other, rows)
    snaps, lines = snap[...], jnp.concatenate([rows[0], rows[1]], axis=1)
    found, penalty = inverse(exact(snaps.T, snaps) * exact(lines.T, lines), state)
    inv[...] = found
    pen[...] = jnp.full((8, 128), penalty, F32)


def row_system_kernel(snap, mine, other, inv, pen, gram, state):
    _, _, core, _ = place_of_own()
    gram[pl.ds(pl.multiple_of(core * 128, 128), 128), :] = mine[...]
    gram[pl.ds(pl.multiple_of((1 - core) * 128, 128), 128), :] = other[...]
    snaps = snap[...]
    found, penalty = inverse(exact(snaps.T, snaps) * gram[...], state)
    inv[...] = found
    pen[...] = jnp.full((8, 128), penalty, F32)


def system(kernel, snap, mine, other, scratch):
    return pl.pallas_call(
        kernel,
        in_specs=[VMEM] * 3,
        out_specs=[VMEM] * 2,
        out_shape=[
            jax.ShapeDtypeStruct((RANK, RANK), F32),
            jax.ShapeDtypeStruct((8, 128), F32),
        ],
        scratch_shapes=[pltpu.VMEM(scratch, F32), pltpu.VMEM((2 * RANK, RANK), F32)],
        cost_estimate=pl.CostEstimate(flops=3_000_000_000, bytes_accessed=1_000_000, transcendentals=0),
        compiler_params=room(8),
    )(snap, mine, other)


def admm_update(sums, inv, penalty, factor, dual, new, dual_new):
    new[...] = factor[...]
    dual_new[...] = dual[...]

    def update(step, carry):
        primal, multiplier = new[...], dual_new[...]
        solved = exact(sums[...] + penalty * (primal + multiplier), inv[...])
        primal = jnp.maximum(solved - multiplier, 0.0)
        new[...] = primal
        dual_new[...] = multiplier + primal - solved
        return carry

    lax.fori_loop(0, ADMM_STEPS, update, 0)


def col_kernel(high, low, snap, inv, pen, factor, dual, *refs):
    pieces = refs[:8]
    new, dual_new, keep, send, gram_half = refs[8:13]
    total, mapped, gram = refs[13:]
    z, x, core, _ = place_of_own()
    for side in range(NC):
        for at, flip in enumerate(FLIPS):
            owner = core if side == 0 else 1 - core
            start = pl.multiple_of(owner * 128 + flipped(x, flip) * 32, 32)
            total[pl.ds(start, 32), :] = pieces[side * NX + at][...]
    admm_update(total, inv, pen[0, 0], factor, dual, new, dual_new)
    primal = new[...]
    gram[...] = exact(primal.T, primal)
    gram_half[...] = gram[pl.ds(pl.multiple_of(core * 128, 128), 128), :]
    lines, weights = split(primal), own_weights(snap, z, x, core)
    for k in range(4):
        line = sum(dot3((high[s, k], low[s, k]), lines) * weights[s] for s in range(2))
        for half in range(2):
            mapped[half, pl.ds(k, BAND, stride=4), :] = line[:, 128 * half : 128 * half + 128]
    for shift in range(NX):
        target = lax.rem(x + shift, NX)
        for ref, owner in ((keep, core), (send, 1 - core)):
            for line in range(NZ):
                start = pl.multiple_of(line * 128 + target * 32 + owner * 16, 16)
                for half in range(2):
                    ref[shift, line, :, 128 * half : 128 * half + 128] = mapped[half, pl.ds(start, 16), :]


def col_update(high, low, snap, inv, pen, factor, dual, pieces):
    square = jax.ShapeDtypeStruct((COLS, RANK), F32)
    part = jax.ShapeDtypeStruct((NX, NZ, 16, RANK), F32)
    return pl.pallas_call(
        col_kernel,
        in_specs=[VMEM] * 15,
        out_specs=[VMEM] * 5,
        out_shape=[square, square, part, part, jax.ShapeDtypeStruct((128, RANK), F32)],
        scratch_shapes=[
            pltpu.VMEM((COLS, RANK), F32),
            pltpu.VMEM((2, KEEP, 128), F32),
            pltpu.VMEM((RANK, RANK), F32),
        ],
        cost_estimate=pl.CostEstimate(flops=1_500_000_000, bytes_accessed=5_000_000, transcendentals=0),
        compiler_params=room(14),
        name="col_update",
    )(high, low, snap, inv, pen, factor, dual, *pieces)


def row_kernel(inv, pen, factor, dual, mine, other, new, dual_new, sums):
    sums[...] = mine[...] + other[...]
    admm_update(sums, inv, pen[0, 0], factor, dual, new, dual_new)


def row_update(inv, pen, factor, dual, mine, other):
    own = jax.ShapeDtypeStruct((16, RANK), F32)
    return pl.pallas_call(
        row_kernel,
        in_specs=[VMEM] * 6,
        out_specs=[VMEM] * 2,
        out_shape=[own] * 2,
        scratch_shapes=[pltpu.VMEM((16, RANK), F32)],
        compiler_params=room(4),
        name="row_update",
    )(inv, pen, factor, dual, mine, other)


def shifted(array, axis, size, by):
    return lax.ppermute(array, axis, [(i, (i + by) % size) for i in range(size)])


def swapped(array, axis, flip):
    return lax.ppermute(array, axis, [(i, i ^ flip) for i in range(4)])


def sum_kernel(count, *refs):
    total = refs[0][...]
    for ref in refs[1:count]:
        total = total + ref[...]
    outs = refs[count:]
    for at, out in enumerate(outs):
        share = total.shape[0] // len(outs)
        own = total if len(outs) == 1 else total[at * share : (at + 1) * share]
        out[...] = own.reshape(out.shape)


def summed(parts, shape, count=1):
    return pl.pallas_call(
        functools.partial(sum_kernel, len(parts)),
        in_specs=[VMEM] * len(parts),
        out_specs=[VMEM] * count,
        out_shape=[jax.ShapeDtypeStruct(shape, F32)] * count,
        compiler_params=room(8),
        name="summed",
    )(*parts)


def spread_kernel(count, *refs):
    total = refs[0][...]
    for ref in refs[1:count]:
        total = total + ref[...]
    for at in range(refs[count].shape[0]):
        refs[count][at] = total


def copied_along(parts, axes, size):
    whole = pl.pallas_call(
        functools.partial(spread_kernel, len(parts)),
        in_specs=[VMEM] * len(parts),
        out_specs=VMEM,
        out_shape=jax.ShapeDtypeStruct((size, *parts[0].shape), F32),
        compiler_params=room(8),
        name="spread",
    )(*parts)
    return lax.all_to_all(whole, axes, 0, 0, tiled=True)


def fold_kernel(block, out):
    half = [block[at] + block[at + 1] for at in range(0, NZ, 2)]
    out[...] = (half[0] + half[1]) + (half[2] + half[3])


def folded(block):
    return pl.pallas_call(
        fold_kernel,
        in_specs=[VMEM],
        out_specs=VMEM,
        out_shape=jax.ShapeDtypeStruct(block.shape[1:], F32),
        compiler_params=room(4),
        name="folded",
    )(block)


def body(snapshots, snap_factor, row_factor, col_factor, row_dual, col_dual):
    mine = copied_along([row_factor], ("z", "x"), NZ * NX)
    high, low, high_t, low_t = dct(snapshots)
    mine, high_t = lax.optimization_barrier((mine, high_t))
    other = shifted(mine, "c", NC, 1)
    keep, send = totals(high_t, low_t, snap_factor, mine, other)
    inv, pen = system(col_system_kernel, snap_factor, mine, other, (2, KEEP, 128))
    line = (32, RANK)
    near, far = summed([keep, shifted(send, "c", NC, 1)], (2, *line), 2)
    near, far = summed([near, swapped(far, "x", 1)], line, 2)
    chunk = copied_along([near, swapped(far, "x", 3)], "z", NZ)
    chunk, pen = lax.optimization_barrier((chunk, pen))
    chunk = folded(chunk)
    across = swapped(chunk, "x", 3)
    pieces = [chunk, across, swapped(chunk, "x", 1), swapped(across, "x", 1)]
    pieces = pieces + [shifted(piece, "c", NC, 1) for piece in pieces]
    col_new, col_dual_new, keep, send, gram_half = col_update(
        high, low, snap_factor, inv, pen, col_factor, col_dual, pieces
    )
    blocks = summed([keep, shifted(send, "c", NC, 1)], (NZ, 16, RANK), NX)
    moved = []
    for by in range(1, NX):
        moved.append(shifted(blocks[by], "x", NX, by))
    gram_near = swapped(gram_half, "y", 1)
    gram_near = summed([gram_half, gram_near], gram_half.shape)[0]
    gram_mine = summed([gram_near, swapped(gram_near, "y", 3)], gram_half.shape)[0]
    gram_other = shifted(gram_mine, "c", NC, 1)
    inv, pen = system(row_system_kernel, snap_factor, gram_mine, gram_other, (RANK, RANK))
    block = summed([blocks[0], *moved], (NZ, 16, RANK))[0]
    block = lax.all_to_all(block, "z", 0, 0, tiled=True)
    block, pen = lax.optimization_barrier((block, pen))
    mine = folded(block)
    near = summed([mine, swapped(mine, "y", 1)], mine.shape)[0]
    row_new, row_dual_new = row_update(
        inv, pen, row_factor, row_dual, near, swapped(near, "y", 3)
    )
    return row_new, col_new, row_dual_new, col_dual_new


def solution(mesh):
    fine = Mesh(mesh.devices.reshape(NZ, NX, NC, NY), ("z", "x", "c", "y"))
    return jax.shard_map(
        body,
        mesh=fine,
        in_specs=(
            P(WIDE, None, "y"),
            P(),
            P(WIDE, None),
            P("y", None),
            P(WIDE, None),
            P("y", None),
        ),
        out_specs=(P(WIDE, None), P("y", None), P(WIDE, None), P("y", None)),
        check_vma=False,
    )
```

```python
import functools
import math

import jax
import jax.numpy as jnp
import numpy as np
from jax import lax
from jax.experimental import pallas as pl
from jax.experimental.pallas import tpu as pltpu
from jax.sharding import Mesh
from jax.sharding import PartitionSpec as P


ROWS = 4096
KEEP = 1024
RANK = 256
COLS = 256
ADMM_STEPS = 3
PART = ROWS // 4
BAND = KEEP // 4
HALF = BAND // 2
STEP = 256
NZ, NX, NC, NY = 8, 4, 2, 4
WIDE = ("z", "x", "c")
F32 = jnp.float32
BF16 = jnp.bfloat16
VMEM = pl.BlockSpec(memory_space=pltpu.VMEM)


def twiddles():
    odd = 2 * np.arange(STEP)[None, :] + 1
    half, group, low = np.meshgrid(np.arange(2), np.arange(32), np.arange(4), indexing="ij")
    degree = (8 * group + 4 * half + low).reshape(BAND, 1)
    scale = math.sqrt(2.0 / ROWS)
    angles = np.pi * odd * degree / 2048, np.pi * odd * (2 * degree + 1) / 4096
    weight = np.where(degree == 0, math.sqrt(1.0 / ROWS), scale), scale
    base = [w * f(a) for w, a in zip(weight, angles) for f in (np.cos, np.sin)]
    lanes = np.ones((1, 128))
    eight = np.arange(8)[:, None] * lanes
    near = np.stack([np.arange(8)[:, None] % 4 * lanes, np.arange(8)[:, None] % 4 * lanes + 4])
    ahead = [f(a) for a in (np.pi * near / 4, np.pi * (2 * near + 1) / 8) for f in (np.cos, np.sin)]
    turn = np.pi * (2 * eight + 1) / 8192
    tables = np.stack(base), np.concatenate([*ahead, [np.cos(turn), np.sin(turn)]])
    return [jnp.asarray(table.astype(np.float32)) for table in tables]


def room(mebibytes):
    return pltpu.CompilerParams(vmem_limit_bytes=mebibytes * 2**20)


def split(value):
    high = value.astype(BF16)
    return high, (value - high.astype(F32)).astype(BF16)


def dot(a, b):
    return jnp.dot(a, b, preferred_element_type=F32)


def dot3(a, b):
    return dot(a[0], b[0]) + (dot(a[1], b[0]) + dot(a[0], b[1]))


def exact(a, b):
    return jnp.dot(a, b, precision=lax.Precision.HIGHEST, preferred_element_type=F32)


def twice(value):
    return jnp.concatenate([value, value], axis=1)


def turned(ref, s):
    index = 7 - lax.broadcasted_iota(jnp.int32, (8, COLS), 0)
    tiles = []
    for t in range(STEP // 8):
        tile = ref[s, STEP - 8 * (t + 1) : STEP - 8 * t, :]
        tiles.append(jnp.take_along_axis(tile, index, axis=0, mode="promise_in_bounds"))
    return jnp.concatenate(tiles, axis=0)


def dct_kernel(x0, x1, x2, x3, *refs):
    base, ahead, keep, send = refs[:4]
    held, rotated, total = refs[4], refs[5:7], refs[7]
    step = pl.program_id(0)

    @pl.when(step == 0)
    def _():
        total[...] = jnp.zeros_like(total)
        held[...] = base[...]
        cos, sin = ahead[8], ahead[9]
        for t in range(STEP // 8):
            by_cos, by_sin = math.cos(math.pi * t / 512), math.sin(math.pi * t / 512)
            rotated[0][8 * t : 8 * t + 8, :] = cos * by_cos - sin * by_sin
            rotated[1][8 * t : 8 * t + 8, :] = sin * by_cos + cos * by_sin

    @pl.when(step > 0)
    def _():
        for pair in range(2):
            cos, sin = held[2 * pair], held[2 * pair + 1]
            by_cos, by_sin = (
                jnp.concatenate([twice(ahead[at])] * 16 + [twice(ahead[at + 1])] * 16, axis=0)
                for at in (4 * pair, 4 * pair + 2)
            )
            held[2 * pair] = cos * by_cos - sin * by_sin
            held[2 * pair + 1] = sin * by_cos + cos * by_sin
        cos, sin = rotated[0][...], rotated[1][...]
        by_cos, by_sin = math.cos(math.pi / 16), math.sin(math.pi / 16)
        rotated[0][...] = cos * by_cos - sin * by_sin
        rotated[1][...] = sin * by_cos + cos * by_sin

    plain, even, odd = split(held[0]), split(held[2]), split(held[3])
    cos, sin = twice(rotated[0][...]), twice(rotated[1][...])
    for s in range(2):
        first, third = x0[s], x2[s]
        second, fourth = turned(x1, s), turned(x3, s)
        outer, inner = first + fourth, second + third
        v, w = first - fourth, second - third
        total[s, 0] += dot3(plain, split(outer + inner))
        total[s, 2] += dot3(even, split(outer - inner))
        p = dot3(even, split(v * cos - w * sin))
        q = dot3(odd, split(v * sin + w * cos))
        total[s, 1] += p + q
        total[s, 3] += p - q

    @pl.when(step == pl.num_programs(0) - 1)
    def _():
        core = lax.axis_index("c")
        for ref, owner in ((keep, core), (send, 1 - core)):
            for s in range(2):
                for k in range(4):
                    ref[s, k] = total[s, k, pl.ds(pl.multiple_of(owner * HALF, HALF), HALF), :]


def dct(snapshots):
    tables = twiddles()
    steps = PART // STEP
    block = (2, STEP, COLS)
    turn = pltpu.VMEM((STEP, 128), F32)
    half = jax.ShapeDtypeStruct((2, 4, HALF, COLS), F32)

    def whole(shape):
        return pl.BlockSpec(shape, lambda i: (0,) * len(shape))

    return pl.pallas_call(
        dct_kernel,
        grid=(steps,),
        in_specs=[
            pl.BlockSpec(block, lambda i: (0, i, 0)),
            pl.BlockSpec(block, lambda i: (0, 2 * steps - 1 - i, 0)),
            pl.BlockSpec(block, lambda i: (0, 2 * steps + i, 0)),
            pl.BlockSpec(block, lambda i: (0, 4 * steps - 1 - i, 0)),
        ]
        + [whole(table.shape) for table in tables],
        out_specs=[whole(half.shape)] * 2,
        out_shape=[half] * 2,
        scratch_shapes=[
            pltpu.VMEM((4, BAND, STEP), F32),
            turn,
            turn,
            pltpu.VMEM((2, 4, BAND, COLS), F32),
        ],
        cost_estimate=pl.CostEstimate(flops=7_000_000_000, bytes_accessed=13_000_000, transcendentals=0),
        compiler_params=room(46),
        name="dct",
    )(*([snapshots] * 4), *tables)


def place_of_own():
    return tuple(lax.axis_index(name) for name in ("z", "x", "c", "y"))


def own_weights(snap, z, x, core):
    chip = (z * NX + x) * 4
    return [snap[pl.ds(chip + 2 * owner + s, 1), :] for owner in (core, 1 - core) for s in range(2)]


def prepare_kernel(own, other, snap, high, low, high_t, low_t, weights):
    z, x, core, _ = place_of_own()
    weights[...] = jnp.concatenate(own_weights(snap, z, x, core) * 2, axis=0)
    for s in range(4):
        source = own if s < 2 else other
        for k in range(4):
            value = source[s % 2, k]
            high[s, k], low[s, k] = split(value)
            place = slice(HALF * k, HALF * (k + 1))
            high_t[s, :, place], low_t[s, :, place] = split(value.T)


def prepare(own, other, snap):
    straight = jax.ShapeDtypeStruct((4, 4, HALF, COLS), BF16)
    crossed = jax.ShapeDtypeStruct((4, COLS, KEEP // 2), BF16)
    return pl.pallas_call(
        prepare_kernel,
        in_specs=[VMEM] * 3,
        out_specs=[VMEM] * 5,
        out_shape=[straight, straight, crossed, crossed, jax.ShapeDtypeStruct((8, RANK), F32)],
        compiler_params=room(12),
        cost_estimate=pl.CostEstimate(flops=10_000_000, bytes_accessed=6_000_000, transcendentals=0),
        name="prepare",
    )(own, other, snap)


def place_rows(x, pieces, rows):
    for shift in range(NX):
        source = lax.rem(x - shift + NX, NX)
        for z in range(NZ):
            start = pl.multiple_of(z * 64 + source * 16, 16)
            for half in range(2):
                rows[half, pl.ds(start, 16), :] = pieces[shift][z, :, 128 * half : 128 * half + 128]


def totals_kernel(high_t, low_t, weights, *refs):
    pieces, (keep, send), (rows, total) = refs[:4], refs[4:6], refs[6:]
    _, x, core, _ = place_of_own()
    place_rows(x, pieces, rows)
    sums = [0.0] * 4
    for k in range(4):
        line = [rows[half, pl.ds(k, HALF, stride=4), :] for half in range(2)]
        lines = split(jnp.concatenate(line, axis=1))
        place = slice(HALF * k, HALF * (k + 1))
        for s in range(4):
            sums[s] += dot3((high_t[s, :, place], low_t[s, :, place]), lines)
    total[...] = sum(part * weights[s : s + 1, :] for s, part in enumerate(sums))
    for shift in range(NX):
        target = lax.rem(x + shift, NX)
        for ref, owner in ((keep, core), (send, 1 - core)):
            start = pl.multiple_of(owner * 128 + target * 32, 32)
            ref[shift] = total[pl.ds(start, 32), :]


def totals(high_t, low_t, weights, pieces):
    part = jax.ShapeDtypeStruct((NX, 32, RANK), F32)
    return pl.pallas_call(
        totals_kernel,
        in_specs=[VMEM] * 7,
        out_specs=[VMEM] * 2,
        out_shape=[part] * 2,
        scratch_shapes=[pltpu.VMEM((2, KEEP // 2, 128), F32), pltpu.VMEM((COLS, RANK), F32)],
        compiler_params=room(12),
        cost_estimate=pl.CostEstimate(flops=800_000_000, bytes_accessed=4_000_000, transcendentals=0),
        name="totals",
    )(high_t, low_t, weights, *pieces)


def row_gram_kernel(*refs):
    pieces, out, rows = refs[:4], refs[4], refs[5]
    place_rows(lax.axis_index("x"), pieces, rows)
    lines = jnp.concatenate([rows[0], rows[1]], axis=1)
    out[...] = exact(lines.T, lines)


def row_gram(pieces):
    return pl.pallas_call(
        row_gram_kernel,
        in_specs=[VMEM] * 4,
        out_specs=VMEM,
        out_shape=jax.ShapeDtypeStruct((RANK, RANK), F32),
        scratch_shapes=[pltpu.VMEM((2, KEEP // 2, 128), F32)],
        compiler_params=room(8),
        cost_estimate=pl.CostEstimate(flops=400_000_000, bytes_accessed=800_000, transcendentals=0),
        name="row_gram",
    )(*pieces)


def inverse(gram, state):
    eye = (
        lax.broadcasted_iota(jnp.int32, (RANK, RANK), 0)
        == lax.broadcasted_iota(jnp.int32, (RANK, RANK), 1)
    ).astype(F32)
    penalty = jnp.sum(gram * eye) / RANK
    system = gram / penalty + eye
    middle = 2.0 / (1.0 + 257.0)
    state[:RANK] = middle * eye
    state[RANK:] = eye - middle * system

    def double(step, reach):
        doubled = 2.0 * reach * reach - 1.0
        gain = 2.0 * reach * reach / doubled
        both = state[...]
        product = gain * dot3(split(both), split(both[RANK:]))
        state[:RANK] = gain * both[:RANK] + product[:RANK]
        state[RANK:] = product[RANK:] - (1.0 / doubled) * eye
        return doubled

    lax.fori_loop(0, 6, double, jnp.float32(258.0 / 256.0))
    found = state[:RANK]
    found = found + dot3(split(found), split(eye - exact(system, found)))
    return found / penalty, penalty


FACTOR, DUAL = RANK + 16, RANK + 16 + COLS


def store_system(found, penalty, weights, inv):
    inv[:RANK] = found
    inv[RANK : RANK + 8] = jnp.full((8, RANK), penalty, F32)
    inv[RANK + 8 : FACTOR] = weights[...]


def col_system_kernel(snap, weights, mine, other, factor, dual, inv, gram, state):
    inv[FACTOR:DUAL] = factor[...]
    inv[DUAL:] = dual[...]
    snaps = snap[...]
    gram[...] = exact(snaps.T, snaps) * (mine[...] + other[...])
    store_system(*inverse(gram[...], state), weights, inv)


def row_system_kernel(snap, weights, mine, other, inv, gram, state):
    core = lax.axis_index("c")
    gram[pl.ds(pl.multiple_of(core * 128, 128), 128), :] = mine[...]
    gram[pl.ds(pl.multiple_of((1 - core) * 128, 128), 128), :] = other[...]
    snaps = snap[...]
    store_system(*inverse(exact(snaps.T, snaps) * gram[...], state), weights, inv)


def system(kernel, rows, *args):
    return pl.pallas_call(
        kernel,
        in_specs=[VMEM] * len(args),
        out_specs=VMEM,
        out_shape=jax.ShapeDtypeStruct((rows, RANK), F32),
        scratch_shapes=[pltpu.VMEM((RANK, RANK), F32), pltpu.VMEM((2 * RANK, RANK), F32)],
        cost_estimate=pl.CostEstimate(flops=3_000_000_000, bytes_accessed=1_000_000, transcendentals=0),
        compiler_params=room(8),
    )(*args)


def admm_update(sums, inv, new, dual_new):
    penalty = inv[RANK, 0]

    def update(step, carry):
        primal, multiplier = new[...], dual_new[...]
        solved = exact(sums[...] + penalty * (primal + multiplier), inv[:RANK])
        primal = jnp.maximum(solved - multiplier, 0.0)
        new[...] = primal
        dual_new[...] = multiplier + primal - solved
        return carry

    lax.fori_loop(0, ADMM_STEPS, update, 0)


def col_kernel(*refs):
    sources, inv, pieces = refs[:2], refs[2], refs[3:11]
    new, dual_new, gram_half, blocks = refs[11], refs[12], refs[13], refs[14:18]
    total, mapped, gram, high, low, sems = refs[18:]
    _, x, core, _ = place_of_own()
    copies = [
        pltpu.make_async_copy(source, target, sems.at[at])
        for at, (source, target) in enumerate(zip(sources, (high, low)))
    ]
    for copy in copies:
        copy.start()
    for side in range(NC):
        for shift in range(NX):
            source = lax.rem(x - shift + NX, NX)
            owner = core if side == 0 else 1 - core
            start = pl.multiple_of(owner * 128 + source * 32, 32)
            total[pl.ds(start, 32), :] = pieces[side * NX + shift][...]
    new[...] = inv[FACTOR:DUAL]
    dual_new[...] = inv[DUAL:]
    admm_update(total, inv, new, dual_new)
    primal = new[...]
    gram[...] = exact(primal.T, primal)
    gram_half[...] = gram[pl.ds(pl.multiple_of(core * 128, 128), 128), :]
    lines, weights = split(primal), inv[RANK + 8 : FACTOR]
    for copy in copies:
        copy.wait()
    for k in range(4):
        line = sum(dot3((high[s, k], low[s, k]), lines) * weights[s : s + 1] for s in range(4))
        for half in range(2):
            mapped[half, pl.ds(k, HALF, stride=4), :] = line[:, 128 * half : 128 * half + 128]
    for shift, block in enumerate(blocks):
        target = lax.rem(x + shift, NX)
        for row in range(NZ):
            start = pl.multiple_of(row * 64 + target * 16, 16)
            for half in range(2):
                block[row, :, 128 * half : 128 * half + 128] = mapped[half, pl.ds(start, 16), :]


def col_update(high, low, inv, pieces):
    square = jax.ShapeDtypeStruct((COLS, RANK), F32)
    block = jax.ShapeDtypeStruct((NZ, 16, RANK), F32)
    outs = [square, square, jax.ShapeDtypeStruct((128, RANK), F32)] + [block] * NX
    return pl.pallas_call(
        col_kernel,
        in_specs=[pl.BlockSpec(memory_space=pltpu.HBM)] * 2 + [VMEM] * 9,
        out_specs=[VMEM] * len(outs),
        out_shape=outs,
        scratch_shapes=[
            pltpu.VMEM((COLS, RANK), F32),
            pltpu.VMEM((2, KEEP // 2, 128), F32),
            pltpu.VMEM((RANK, RANK), F32),
            pltpu.VMEM((4, 4, HALF, COLS), BF16),
            pltpu.VMEM((4, 4, HALF, COLS), BF16),
            pltpu.SemaphoreType.DMA((2,)),
        ],
        cost_estimate=pl.CostEstimate(flops=1_500_000_000, bytes_accessed=5_000_000, transcendentals=0),
        compiler_params=room(16),
        name="col_update",
    )(high, low, inv, *pieces)


def gram_sum_kernel(*refs):
    parts, out, held = refs[:4], refs[4], refs[5]
    y = lax.axis_index("y")
    for shift in range(NY):
        held[lax.rem(y - shift + NY, NY)] = parts[shift][...]
    out[...] = (held[0] + held[1]) + (held[2] + held[3])


def gram_sum(parts):
    shape = parts[0].shape
    return pl.pallas_call(
        gram_sum_kernel,
        in_specs=[VMEM] * NY,
        out_specs=VMEM,
        out_shape=jax.ShapeDtypeStruct(shape, F32),
        scratch_shapes=[pltpu.VMEM((NY, *shape), F32)],
        compiler_params=room(4),
        name="gram_sum",
    )(*parts)


def row_kernel(inv, factor, dual, mine, other, new, dual_new, sums):
    sums[...] = mine[...] + other[...]
    new[...] = factor[...]
    dual_new[...] = dual[...]
    admm_update(sums, inv, new, dual_new)


def row_update(inv, factor, dual, mine, other):
    own = jax.ShapeDtypeStruct((16, RANK), F32)
    return pl.pallas_call(
        row_kernel,
        in_specs=[VMEM] * 5,
        out_specs=[VMEM] * 2,
        out_shape=[own] * 2,
        scratch_shapes=[pltpu.VMEM((16, RANK), F32)],
        compiler_params=room(4),
        name="row_update",
    )(inv, factor, dual, mine, other)


def shifted(array, axis, size, by):
    return lax.ppermute(array, axis, [(i, (i + by) % size) for i in range(size)])


def swapped(array, axis, flip):
    return lax.ppermute(array, axis, [(i, i ^ flip) for i in range(4)])


def sum_kernel(count, *refs):
    total = refs[0][...]
    for ref in refs[1:count]:
        total = total + ref[...]
    outs = refs[count:]
    for at, out in enumerate(outs):
        share = total.shape[0] // len(outs)
        own = total if len(outs) == 1 else total[at * share : (at + 1) * share]
        out[...] = own.reshape(out.shape)


def summed(parts, shape, count=1):
    return pl.pallas_call(
        functools.partial(sum_kernel, len(parts)),
        in_specs=[VMEM] * len(parts),
        out_specs=[VMEM] * count,
        out_shape=[jax.ShapeDtypeStruct(shape, F32)] * count,
        compiler_params=room(8),
        name="summed",
    )(*parts)


def spread_kernel(count, *refs):
    total = refs[0][...]
    for ref in refs[1:count]:
        total = total + ref[...]
    for at in range(refs[count].shape[0]):
        refs[count][at] = total


def copied_along(parts, axes, size):
    whole = pl.pallas_call(
        functools.partial(spread_kernel, len(parts)),
        in_specs=[VMEM] * len(parts),
        out_specs=VMEM,
        out_shape=jax.ShapeDtypeStruct((size, *parts[0].shape), F32),
        compiler_params=room(8),
        name="spread",
    )(*parts)
    return lax.all_to_all(whole, axes, 0, 0, tiled=True)


def fold_kernel(block, out):
    half = [block[at] + block[at + 1] for at in range(0, NZ, 2)]
    out[...] = (half[0] + half[1]) + (half[2] + half[3])


def folded(block):
    return pl.pallas_call(
        fold_kernel,
        in_specs=[VMEM],
        out_specs=VMEM,
        out_shape=jax.ShapeDtypeStruct(block.shape[1:], F32),
        compiler_params=room(4),
        name="folded",
    )(block)


def body(snapshots, snap_factor, row_factor, col_factor, row_dual, col_dual):
    mine = copied_along([row_factor], "z", NZ)
    own, send = dct(snapshots)
    mine, own, send = lax.optimization_barrier((mine, own, send))
    lines = [mine] + [shifted(mine, "x", NX, by) for by in range(1, NX)]
    high, low, high_t, low_t, weights = prepare(own, shifted(send, "c", NC, 1), snap_factor)
    keep, send = totals(high_t, low_t, weights, lines)
    gram = row_gram(lines)
    other = shifted(gram, "c", NC, 1)
    args = snap_factor, weights, gram, other
    inv = system(col_system_kernel, DUAL + COLS, *args, col_factor, col_dual)
    parts = summed([keep, shifted(send, "c", NC, 1)], (32, RANK), NX)
    parts = [parts[0]] + [shifted(parts[by], "x", NX, by) for by in range(1, NX)]
    chunk = copied_along(parts, "z", NZ)
    chunk, inv = lax.optimization_barrier((chunk, inv))
    chunk = folded(chunk)
    pieces = [chunk] + [shifted(chunk, "x", NX, by) for by in range(1, NX)]
    pieces = pieces + [shifted(piece, "c", NC, 1) for piece in pieces]
    col_new, col_dual_new, gram_half, *blocks = col_update(
        high, low, inv, pieces
    )
    grams = [gram_half]
    for by in range(1, NX):
        blocks[by] = shifted(blocks[by], "x", NX, by)
    for by in range(1, NY):
        grams.append(shifted(gram_half, "y", NY, by))
    block = summed(blocks, (NZ, 16, RANK))[0]
    _, *grams = lax.optimization_barrier((block, *grams))
    gram_mine = gram_sum(grams)
    other = shifted(gram_mine, "c", NC, 1)
    args = snap_factor, weights, gram_mine, other
    inv = system(row_system_kernel, FACTOR, *args)
    block = lax.all_to_all(block, "z", 0, 0, tiled=True)
    block, inv = lax.optimization_barrier((block, inv))
    mine = folded(block)
    near = summed([mine, swapped(mine, "y", 1)], mine.shape)[0]
    row_new, row_dual_new = row_update(inv, row_factor, row_dual, near, swapped(near, "y", 3))
    return row_new, col_new, row_dual_new, col_dual_new


def solution(mesh):
    fine = Mesh(mesh.devices.reshape(NZ, NX, NC, NY), ("z", "x", "c", "y"))
    return jax.shard_map(
        body,
        mesh=fine,
        in_specs=(
            P(WIDE, None, "y"),
            P(),
            P(WIDE, None),
            P("y", None),
            P(WIDE, None),
            P("y", None),
        ),
        out_specs=(P(WIDE, None), P("y", None), P(WIDE, None), P("y", None)),
        check_vma=False,
    )
```

```python
import functools
import math

import jax
import jax.numpy as jnp
import numpy as np
from jax import lax
from jax.experimental import pallas as pl
from jax.experimental.pallas import tpu as pltpu
from jax.sharding import Mesh
from jax.sharding import PartitionSpec as P


ROWS = 4096
KEEP = 1024
RANK = 256
COLS = 256
ADMM_STEPS = 3
PART = ROWS // 4
BAND = KEEP // 4
HALF = BAND // 2
STEP = 256
NZ, NX, NC, NY = 8, 4, 2, 4
WIDE = ("z", "x", "c")
F32 = jnp.float32
BF16 = jnp.bfloat16
VMEM = pl.BlockSpec(memory_space=pltpu.VMEM)


def twiddles():
    odd = 2 * np.arange(STEP)[None, :] + 1
    sizes = (NC, NX, NZ, 4)
    half, x, z, low = np.meshgrid(*map(np.arange, sizes), indexing="ij")
    degree = (8 * (NX * z + x) + 4 * half + low).reshape(BAND, 1)
    scale = math.sqrt(2.0 / ROWS)
    angles = np.pi * odd * degree / 2048, np.pi * odd * (2 * degree + 1) / 4096
    weight = np.where(degree == 0, math.sqrt(1.0 / ROWS), scale), scale
    base = [w * f(a) for w, a in zip(weight, angles) for f in (np.cos, np.sin)]
    lanes = np.ones((1, 128))
    eight = np.arange(8)[:, None] * lanes
    near = np.stack([np.arange(8)[:, None] % 4 * lanes, np.arange(8)[:, None] % 4 * lanes + 4])
    ahead = [f(a) for a in (np.pi * near / 4, np.pi * (2 * near + 1) / 8) for f in (np.cos, np.sin)]
    turn = np.pi * (2 * eight + 1) / 8192
    tables = np.stack(base), np.concatenate([*ahead, [np.cos(turn), np.sin(turn)]])
    return [jnp.asarray(table.astype(np.float32)) for table in tables]


def room(mebibytes):
    return pltpu.CompilerParams(vmem_limit_bytes=mebibytes * 2**20)


def split(value):
    high = value.astype(BF16)
    return high, (value - high.astype(F32)).astype(BF16)


def dot(a, b):
    return jnp.dot(a, b, preferred_element_type=F32)


def dot3(a, b):
    return dot(a[0], b[0]) + (dot(a[1], b[0]) + dot(a[0], b[1]))


def exact(a, b):
    return jnp.dot(a, b, precision=lax.Precision.HIGHEST, preferred_element_type=F32)


def twice(value):
    return jnp.concatenate([value, value], axis=1)


def turned(ref, s):
    index = 7 - lax.broadcasted_iota(jnp.int32, (8, COLS), 0)
    tiles = []
    for t in range(STEP // 8):
        tile = ref[s, STEP - 8 * (t + 1) : STEP - 8 * t, :]
        tiles.append(jnp.take_along_axis(tile, index, axis=0, mode="promise_in_bounds"))
    return jnp.concatenate(tiles, axis=0)


def dct_kernel(x0, x1, x2, x3, *refs):
    base, ahead, keep, send = refs[:4]
    held, rotated, total = refs[4], refs[5:7], refs[7]
    step = pl.program_id(0)

    @pl.when(step == 0)
    def _():
        total[...] = jnp.zeros_like(total)
        held[...] = base[...]
        cos, sin = ahead[8], ahead[9]
        for t in range(STEP // 8):
            by_cos, by_sin = math.cos(math.pi * t / 512), math.sin(math.pi * t / 512)
            rotated[0][8 * t : 8 * t + 8, :] = cos * by_cos - sin * by_sin
            rotated[1][8 * t : 8 * t + 8, :] = sin * by_cos + cos * by_sin

    @pl.when(step > 0)
    def _():
        for pair in range(2):
            cos, sin = held[2 * pair], held[2 * pair + 1]
            by_cos, by_sin = (
                jnp.concatenate([twice(ahead[at])] * 16 + [twice(ahead[at + 1])] * 16, axis=0)
                for at in (4 * pair, 4 * pair + 2)
            )
            held[2 * pair] = cos * by_cos - sin * by_sin
            held[2 * pair + 1] = sin * by_cos + cos * by_sin
        cos, sin = rotated[0][...], rotated[1][...]
        by_cos, by_sin = math.cos(math.pi / 16), math.sin(math.pi / 16)
        rotated[0][...] = cos * by_cos - sin * by_sin
        rotated[1][...] = sin * by_cos + cos * by_sin

    plain, even, odd = split(held[0]), split(held[2]), split(held[3])
    cos, sin = twice(rotated[0][...]), twice(rotated[1][...])
    for s in range(2):
        first, third = x0[s], x2[s]
        second, fourth = turned(x1, s), turned(x3, s)
        outer, inner = first + fourth, second + third
        v, w = first - fourth, second - third
        total[s, 0] += dot3(plain, split(outer + inner))
        total[s, 2] += dot3(even, split(outer - inner))
        p = dot3(even, split(v * cos - w * sin))
        q = dot3(odd, split(v * sin + w * cos))
        total[s, 1] += p + q
        total[s, 3] += p - q

    @pl.when(step == pl.num_programs(0) - 1)
    def _():
        core = lax.axis_index("c")
        for ref, owner in ((keep, core), (send, 1 - core)):
            for s in range(2):
                for k in range(4):
                    ref[s, k] = total[s, k, pl.ds(pl.multiple_of(owner * HALF, HALF), HALF), :]


def dct(snapshots):
    tables = twiddles()
    steps = PART // STEP
    block = (2, STEP, COLS)
    turn = pltpu.VMEM((STEP, 128), F32)
    half = jax.ShapeDtypeStruct((2, 4, HALF, COLS), F32)

    def whole(shape):
        return pl.BlockSpec(shape, lambda i: (0,) * len(shape))

    return pl.pallas_call(
        dct_kernel,
        grid=(steps,),
        in_specs=[
            pl.BlockSpec(block, lambda i: (0, i, 0)),
            pl.BlockSpec(block, lambda i: (0, 2 * steps - 1 - i, 0)),
            pl.BlockSpec(block, lambda i: (0, 2 * steps + i, 0)),
            pl.BlockSpec(block, lambda i: (0, 4 * steps - 1 - i, 0)),
        ]
        + [whole(table.shape) for table in tables],
        out_specs=[whole(half.shape)] * 2,
        out_shape=[half] * 2,
        scratch_shapes=[
            pltpu.VMEM((4, BAND, STEP), F32),
            turn,
            turn,
            pltpu.VMEM((2, 4, BAND, COLS), F32),
        ],
        cost_estimate=pl.CostEstimate(flops=7_000_000_000, bytes_accessed=13_000_000, transcendentals=0),
        compiler_params=room(46),
        name="dct",
    )(*([snapshots] * 4), *tables)


def place_of_own():
    return tuple(lax.axis_index(name) for name in ("z", "x", "c", "y"))


def own_weights(snap, z, x, core):
    chip = (z * NX + x) * 4
    return [snap[pl.ds(chip + 2 * owner + s, 1), :] for owner in (core, 1 - core) for s in range(2)]


def prepare_kernel(own, other, snap, high_t, low_t, weights, *blocks):
    z, x, core, _ = place_of_own()
    lines = [own_weights(snap, z, lax.rem(x - shift + NX, NX), core) for shift in range(NX)]
    weights[...] = jnp.concatenate(sum(lines, []), axis=0)
    for s in range(4):
        source = own if s < 2 else other
        for k in range(4):
            place = slice(HALF * k, HALF * (k + 1))
            high_t[s, :, place], low_t[s, :, place] = split(source[s % 2, k].T)
            for shift, block in enumerate(blocks):
                start = pl.multiple_of(lax.rem(x + shift, NX) * 32, 32)
                block[s, k] = source[s % 2, k, pl.ds(start, 32), :]


def prepare(own, other, snap):
    crossed = jax.ShapeDtypeStruct((4, COLS, KEEP // 2), BF16)
    block = jax.ShapeDtypeStruct((4, 4, 32, COLS), F32)
    outs = [crossed, crossed, jax.ShapeDtypeStruct((16, RANK), F32)] + [block] * NX
    return pl.pallas_call(
        prepare_kernel,
        in_specs=[VMEM] * 3,
        out_specs=[VMEM] * len(outs),
        out_shape=outs,
        compiler_params=room(12),
        cost_estimate=pl.CostEstimate(flops=10_000_000, bytes_accessed=6_000_000, transcendentals=0),
        name="prepare",
    )(own, other, snap)


def place_rows(x, pieces, rows):
    for shift in range(NX):
        source = lax.rem(x - shift + NX, NX)
        for z in range(NZ):
            start = pl.multiple_of(source * 128 + z * 16, 16)
            for half in range(2):
                rows[half, pl.ds(start, 16), :] = pieces[shift][z, :, 128 * half : 128 * half + 128]


def totals_kernel(high_t, low_t, weights, *refs):
    pieces, (keep, send), (rows, total) = refs[:4], refs[4:6], refs[6:]
    _, x, core, _ = place_of_own()
    place_rows(x, pieces, rows)
    sums = [0.0] * 4
    for k in range(4):
        line = [rows[half, pl.ds(k, HALF, stride=4), :] for half in range(2)]
        lines = split(jnp.concatenate(line, axis=1))
        place = slice(HALF * k, HALF * (k + 1))
        for s in range(4):
            sums[s] += dot3((high_t[s, :, place], low_t[s, :, place]), lines)
    total[...] = sum(part * weights[s : s + 1, :] for s, part in enumerate(sums))
    for shift in range(NX):
        target = lax.rem(x + shift, NX)
        for ref, owner in ((keep, core), (send, 1 - core)):
            start = pl.multiple_of(owner * 128 + target * 32, 32)
            ref[shift] = total[pl.ds(start, 32), :]


def totals(high_t, low_t, weights, pieces):
    part = jax.ShapeDtypeStruct((NX, 32, RANK), F32)
    return pl.pallas_call(
        totals_kernel,
        in_specs=[VMEM] * 7,
        out_specs=[VMEM] * 2,
        out_shape=[part] * 2,
        scratch_shapes=[pltpu.VMEM((2, KEEP // 2, 128), F32), pltpu.VMEM((COLS, RANK), F32)],
        compiler_params=room(12),
        cost_estimate=pl.CostEstimate(flops=800_000_000, bytes_accessed=4_000_000, transcendentals=0),
        name="totals",
    )(high_t, low_t, weights, *pieces)


def row_gram_kernel(*refs):
    pieces, out, rows = refs[:4], refs[4], refs[5]
    place_rows(lax.axis_index("x"), pieces, rows)
    lines = jnp.concatenate([rows[0], rows[1]], axis=1)
    out[...] = exact(lines.T, lines)


def row_gram(pieces):
    return pl.pallas_call(
        row_gram_kernel,
        in_specs=[VMEM] * 4,
        out_specs=VMEM,
        out_shape=jax.ShapeDtypeStruct((RANK, RANK), F32),
        scratch_shapes=[pltpu.VMEM((2, KEEP // 2, 128), F32)],
        compiler_params=room(8),
        cost_estimate=pl.CostEstimate(flops=400_000_000, bytes_accessed=800_000, transcendentals=0),
        name="row_gram",
    )(*pieces)


def inverse(gram, state):
    eye = (
        lax.broadcasted_iota(jnp.int32, (RANK, RANK), 0)
        == lax.broadcasted_iota(jnp.int32, (RANK, RANK), 1)
    ).astype(F32)
    penalty = jnp.sum(gram * eye) / RANK
    system = gram / penalty + eye
    middle = 2.0 / (1.0 + 257.0)
    state[:RANK] = middle * eye
    state[RANK:] = eye - middle * system

    def double(step, reach):
        doubled = 2.0 * reach * reach - 1.0
        gain = 2.0 * reach * reach / doubled
        both = state[...]
        product = gain * dot3(split(both), split(both[RANK:]))
        state[:RANK] = gain * both[:RANK] + product[:RANK]
        state[RANK:] = product[RANK:] - (1.0 / doubled) * eye
        return doubled

    lax.fori_loop(0, 6, double, jnp.float32(258.0 / 256.0))
    found = state[:RANK]
    found = found + dot3(split(found), split(eye - exact(system, found)))
    return found / penalty, penalty


FACTOR, DUAL = RANK + 24, RANK + 24 + COLS


def store_system(found, penalty, weights, inv):
    inv[:RANK] = found
    inv[RANK : RANK + 8] = jnp.full((8, RANK), penalty, F32)
    inv[RANK + 8 : FACTOR] = weights[...]


def col_system_kernel(snap, weights, mine, other, factor, dual, inv, gram, state):
    inv[FACTOR:DUAL] = factor[...]
    inv[DUAL:] = dual[...]
    snaps = snap[...]
    gram[...] = exact(snaps.T, snaps) * (mine[...] + other[...])
    store_system(*inverse(gram[...], state), weights, inv)


def row_system_kernel(snap, weights, mine, other, inv, gram, state):
    core = lax.axis_index("c")
    gram[pl.ds(pl.multiple_of(core * 128, 128), 128), :] = mine[...]
    gram[pl.ds(pl.multiple_of((1 - core) * 128, 128), 128), :] = other[...]
    snaps = snap[...]
    store_system(*inverse(exact(snaps.T, snaps) * gram[...], state), weights, inv)


def system(kernel, rows, *args):
    return pl.pallas_call(
        kernel,
        in_specs=[VMEM] * len(args),
        out_specs=VMEM,
        out_shape=jax.ShapeDtypeStruct((rows, RANK), F32),
        scratch_shapes=[pltpu.VMEM((RANK, RANK), F32), pltpu.VMEM((2 * RANK, RANK), F32)],
        cost_estimate=pl.CostEstimate(flops=3_000_000_000, bytes_accessed=1_000_000, transcendentals=0),
        compiler_params=room(8),
    )(*args)


def admm_update(sums, inv, new, dual_new):
    penalty = inv[RANK, 0]

    def update(step, carry):
        primal, multiplier = new[...], dual_new[...]
        solved = exact(sums[...] + penalty * (primal + multiplier), inv[:RANK])
        primal = jnp.maximum(solved - multiplier, 0.0)
        new[...] = primal
        dual_new[...] = multiplier + primal - solved
        return carry

    lax.fori_loop(0, ADMM_STEPS, update, 0)


def col_kernel(*refs):
    sources, inv, pieces = refs[:4], refs[4], refs[5:13]
    new, dual_new, gram_half, block = refs[13:17]
    total, mapped, gram, held, sems = refs[17:]
    _, x, core, _ = place_of_own()
    copies = [
        pltpu.make_async_copy(source, held.at[at], sems.at[at])
        for at, source in enumerate(sources)
    ]
    for copy in copies:
        copy.start()
    for side in range(NC):
        for shift in range(NX):
            source = lax.rem(x - shift + NX, NX)
            owner = core if side == 0 else 1 - core
            start = pl.multiple_of(owner * 128 + source * 32, 32)
            total[pl.ds(start, 32), :] = pieces[side * NX + shift][...]
    new[...] = inv[FACTOR:DUAL]
    dual_new[...] = inv[DUAL:]
    admm_update(total, inv, new, dual_new)
    primal = new[...]
    gram[...] = exact(primal.T, primal)
    gram_half[...] = gram[pl.ds(pl.multiple_of(core * 128, 128), 128), :]
    lines, weights = split(primal), inv[RANK + 8 : FACTOR]
    for copy in copies:
        copy.wait()
    sums = 0.0
    for shift in range(NX):
        product = dot3(split(held[shift].reshape(512, COLS)), lines)
        for s in range(4):
            at = 4 * shift + s
            sums += product[128 * s : 128 * s + 128] * weights[at : at + 1]
    for k in range(4):
        for half in range(2):
            line = sums[32 * k : 32 * k + 32, 128 * half : 128 * half + 128]
            mapped[half, pl.ds(k, 32, stride=4), :] = line
    for row in range(NZ):
        for half in range(2):
            place = slice(128 * half, 128 * half + 128)
            block[row, :, place] = mapped[half, 16 * row : 16 * row + 16, :]


def col_update(coefficients, inv, pieces):
    square = jax.ShapeDtypeStruct((COLS, RANK), F32)
    block = jax.ShapeDtypeStruct((NZ, 16, RANK), F32)
    outs = [square, square, jax.ShapeDtypeStruct((128, RANK), F32), block]
    return pl.pallas_call(
        col_kernel,
        in_specs=[pl.BlockSpec(memory_space=pltpu.HBM)] * 4 + [VMEM] * 9,
        out_specs=[VMEM] * len(outs),
        out_shape=outs,
        scratch_shapes=[
            pltpu.VMEM((COLS, RANK), F32),
            pltpu.VMEM((2, 128, 128), F32),
            pltpu.VMEM((RANK, RANK), F32),
            pltpu.VMEM((NX, 4, 4, 32, COLS), F32),
            pltpu.SemaphoreType.DMA((4,)),
        ],
        cost_estimate=pl.CostEstimate(flops=1_500_000_000, bytes_accessed=5_000_000, transcendentals=0),
        compiler_params=room(16),
        name="col_update",
    )(*coefficients, inv, *pieces)


def gram_sum_kernel(*refs):
    parts, out, held = refs[:4], refs[4], refs[5]
    y = lax.axis_index("y")
    for shift in range(NY):
        held[lax.rem(y - shift + NY, NY)] = parts[shift][...]
    out[...] = (held[0] + held[1]) + (held[2] + held[3])


def gram_sum(parts):
    shape = parts[0].shape
    return pl.pallas_call(
        gram_sum_kernel,
        in_specs=[VMEM] * NY,
        out_specs=VMEM,
        out_shape=jax.ShapeDtypeStruct(shape, F32),
        scratch_shapes=[pltpu.VMEM((NY, *shape), F32)],
        compiler_params=room(4),
        name="gram_sum",
    )(*parts)


def row_kernel(inv, factor, dual, mine, other, new, dual_new, sums):
    sums[...] = mine[...] + other[...]
    new[...] = factor[...]
    dual_new[...] = dual[...]
    admm_update(sums, inv, new, dual_new)


def row_update(inv, factor, dual, mine, other):
    own = jax.ShapeDtypeStruct((16, RANK), F32)
    return pl.pallas_call(
        row_kernel,
        in_specs=[VMEM] * 5,
        out_specs=[VMEM] * 2,
        out_shape=[own] * 2,
        scratch_shapes=[pltpu.VMEM((16, RANK), F32)],
        compiler_params=room(4),
        name="row_update",
    )(inv, factor, dual, mine, other)


def shifted(array, axis, size, by):
    return lax.ppermute(array, axis, [(i, (i + by) % size) for i in range(size)])


def swapped(array, axis, flip):
    return lax.ppermute(array, axis, [(i, i ^ flip) for i in range(4)])


def sum_kernel(count, *refs):
    total = refs[0][...]
    for ref in refs[1:count]:
        total = total + ref[...]
    outs = refs[count:]
    for at, out in enumerate(outs):
        share = total.shape[0] // len(outs)
        own = total if len(outs) == 1 else total[at * share : (at + 1) * share]
        out[...] = own.reshape(out.shape)


def summed(parts, shape, count=1):
    return pl.pallas_call(
        functools.partial(sum_kernel, len(parts)),
        in_specs=[VMEM] * len(parts),
        out_specs=[VMEM] * count,
        out_shape=[jax.ShapeDtypeStruct(shape, F32)] * count,
        compiler_params=room(8),
        name="summed",
    )(*parts)


def spread_kernel(count, *refs):
    total = refs[0][...]
    for ref in refs[1:count]:
        total = total + ref[...]
    for at in range(refs[count].shape[0]):
        refs[count][at] = total


def copied_along(parts, axes, size):
    whole = pl.pallas_call(
        functools.partial(spread_kernel, len(parts)),
        in_specs=[VMEM] * len(parts),
        out_specs=VMEM,
        out_shape=jax.ShapeDtypeStruct((size, *parts[0].shape), F32),
        compiler_params=room(8),
        name="spread",
    )(*parts)
    return lax.all_to_all(whole, axes, 0, 0, tiled=True)


def fold_kernel(block, out):
    half = [block[at] + block[at + 1] for at in range(0, NZ, 2)]
    out[...] = (half[0] + half[1]) + (half[2] + half[3])


def folded(block):
    return pl.pallas_call(
        fold_kernel,
        in_specs=[VMEM],
        out_specs=VMEM,
        out_shape=jax.ShapeDtypeStruct(block.shape[1:], F32),
        compiler_params=room(4),
        name="folded",
    )(block)


def around(array, axis):
    moved = []
    for by in range(1, 4):
        given = array[by] if isinstance(array, list) else array
        moved.append(shifted(given, axis, 4, by))
    return moved


def update(snapshots, snap_factor, row_factor, col_factor, row_dual, col_dual):
    mine = copied_along([row_factor], "z", NZ)
    own, send = dct(snapshots)
    mine, own, send = lax.optimization_barrier((mine, own, send))
    lines = [mine, *around(mine, "x")]
    high_t, low_t, weights, *blocks = prepare(own, shifted(send, "c", NC, 1), snap_factor)
    keep, send = totals(high_t, low_t, weights, lines)
    gram = row_gram(lines)
    other = shifted(gram, "c", NC, 1)
    args = snap_factor, weights, gram, other
    inv = system(col_system_kernel, DUAL + COLS, *args, col_factor, col_dual)
    parts = list(summed([keep, shifted(send, "c", NC, 1)], (32, RANK), NX))
    chunk = copied_along([parts[0], *around(parts, "x")], "z", NZ)
    coefficients = [blocks[0], *around(list(blocks), "x")]
    chunk, inv = lax.optimization_barrier((chunk, inv))
    chunk = folded(chunk)
    pieces = [chunk, *around(chunk, "x")]
    pieces = pieces + [shifted(piece, "c", NC, 1) for piece in pieces]
    col_new, col_dual_new, gram_half, block = col_update(coefficients, inv, pieces)
    grams = [gram_half, *around(gram_half, "y")]
    gram_mine = gram_sum(grams)
    other = shifted(gram_mine, "c", NC, 1)
    args = snap_factor, weights, gram_mine, other
    inv = system(row_system_kernel, FACTOR, *args)
    block = lax.all_to_all(block, "z", 0, 0, tiled=True)
    block, inv = lax.optimization_barrier((block, inv))
    mine = folded(block)
    near = summed([mine, swapped(mine, "y", 1)], mine.shape)[0]
    row_new, row_dual_new = row_update(inv, row_factor, row_dual, near, swapped(near, "y", 3))
    return row_new, col_new, row_dual_new, col_dual_new


def solution(mesh):
    fine = Mesh(mesh.devices.reshape(NZ, NX, NC, NY), ("z", "x", "c", "y"))
    return jax.shard_map(
        update,
        mesh=fine,
        in_specs=(
            P(WIDE, None, "y"),
            P(),
            P(WIDE, None),
            P("y", None),
            P(WIDE, None),
            P("y", None),
        ),
        out_specs=(P(WIDE, None), P("y", None), P(WIDE, None), P("y", None)),
        check_vma=False,
    )
```

```python
import functools
import math

import jax
import jax.numpy as jnp
import numpy as np
from jax import lax
from jax.experimental import pallas as pl
from jax.experimental.pallas import tpu as pltpu
from jax.sharding import Mesh
from jax.sharding import PartitionSpec as P


ROWS = 4096
KEEP = 1024
RANK = 256
COLS = 256
ADMM_STEPS = 3
PART = ROWS // 4
BAND = KEEP // 4
HALF = BAND // 2
STEP = 256
NZ, NX, NC, NY = 8, 4, 2, 4
WIDE = ("z", "x", "c")
F32 = jnp.float32
BF16 = jnp.bfloat16
VMEM = pl.BlockSpec(memory_space=pltpu.VMEM)


def twiddles():
    odd = 2 * np.arange(STEP)[None, :] + 1
    sizes = (NC, NX, NZ, 4)
    half, x, z, low = np.meshgrid(*map(np.arange, sizes), indexing="ij")
    degree = (8 * (NX * z + x) + 4 * half + low).reshape(BAND, 1)
    scale = math.sqrt(2.0 / ROWS)
    angles = np.pi * odd * degree / 2048, np.pi * odd * (2 * degree + 1) / 4096
    weight = np.where(degree == 0, math.sqrt(1.0 / ROWS), scale), scale
    base = [w * f(a) for w, a in zip(weight, angles) for f in (np.cos, np.sin)]
    lanes = np.ones((1, 128))
    eight = np.arange(8)[:, None] * lanes
    near = np.stack([np.arange(8)[:, None] % 4 * lanes, np.arange(8)[:, None] % 4 * lanes + 4])
    ahead = [f(a) for a in (np.pi * near / 4, np.pi * (2 * near + 1) / 8) for f in (np.cos, np.sin)]
    turn = np.pi * (2 * eight + 1) / 8192
    turns = [np.cos(turn), np.sin(turn)] * 2
    parts = [base, [np.concatenate(part) for part in ahead], turns]
    parts = [np.stack([np.tile(p, (1, STEP // p.shape[1])) for p in part]) for part in parts]
    return jnp.asarray(np.concatenate(parts, axis=1).astype(np.float32))


def room(mebibytes):
    return pltpu.CompilerParams(vmem_limit_bytes=mebibytes * 2**20)


def split(value):
    high = value.astype(BF16)
    return high, (value - high.astype(F32)).astype(BF16)


def dot(a, b):
    return jnp.dot(a, b, preferred_element_type=F32)


def dot3(a, b):
    return dot(a[0], b[0]) + (dot(a[1], b[0]) + dot(a[0], b[1]))


def exact(a, b):
    return jnp.dot(a, b, precision=lax.Precision.HIGHEST, preferred_element_type=F32)


def twice(value):
    return jnp.concatenate([value, value], axis=1)


def turned(ref, s):
    index = 7 - lax.broadcasted_iota(jnp.int32, (8, COLS), 0)
    tiles = []
    for t in range(STEP // 8):
        tile = ref[s, STEP - 8 * (t + 1) : STEP - 8 * t, :]
        tiles.append(jnp.take_along_axis(tile, index, axis=0, mode="promise_in_bounds"))
    return jnp.concatenate(tiles, axis=0)


def dct_kernel(x0, x1, x2, x3, table, keep, send, held, rotated, total):
    step = pl.program_id(0)

    @pl.when(step == 0)
    def _():
        total[...] = jnp.zeros_like(total)
        held[...] = table[:, :BAND]
        cos, sin = table[0, BAND + 16 :, :128], table[1, BAND + 16 :, :128]
        for t in range(STEP // 8):
            by_cos, by_sin = math.cos(math.pi * t / 512), math.sin(math.pi * t / 512)
            rotated[0, 8 * t : 8 * t + 8, :] = cos * by_cos - sin * by_sin
            rotated[1, 8 * t : 8 * t + 8, :] = sin * by_cos + cos * by_sin

    @pl.when(step > 0)
    def _():
        for pair in range(2):
            cos, sin = held[2 * pair], held[2 * pair + 1]
            by_cos, by_sin = (
                jnp.concatenate(
                    [table[at, BAND : BAND + 8]] * 16 + [table[at, BAND + 8 : BAND + 16]] * 16, axis=0
                )
                for at in (2 * pair, 2 * pair + 1)
            )
            held[2 * pair] = cos * by_cos - sin * by_sin
            held[2 * pair + 1] = sin * by_cos + cos * by_sin
        cos, sin = rotated[0], rotated[1]
        by_cos, by_sin = math.cos(math.pi / 16), math.sin(math.pi / 16)
        rotated[0] = cos * by_cos - sin * by_sin
        rotated[1] = sin * by_cos + cos * by_sin

    plain, even, odd = split(held[0]), split(held[2]), split(held[3])
    cos, sin = twice(rotated[0]), twice(rotated[1])
    first, third = x0[0], x2[0]
    second, fourth = turned(x1, 0), turned(x3, 0)
    outer, inner = first + fourth, second + third
    v, w = first - fourth, second - third
    total[0] += dot3(plain, split(outer + inner))
    total[2] += dot3(even, split(outer - inner))
    p = dot3(even, split(v * cos - w * sin))
    q = dot3(odd, split(v * sin + w * cos))
    total[1] += p + q
    total[3] += p - q

    @pl.when(step == pl.num_programs(0) - 1)
    def _():
        core = lax.axis_index("c")
        for ref, owner in ((keep, core), (send, 1 - core)):
            for k in range(4):
                ref[k] = total[k, pl.ds(pl.multiple_of(owner * HALF, HALF), HALF), :]


def dct(snapshots, table, at):
    steps = PART // STEP
    block = (1, STEP, COLS)
    half = jax.ShapeDtypeStruct((4, HALF, COLS), F32)

    def whole(shape):
        return pl.BlockSpec(shape, lambda i: (0,) * len(shape))

    return pl.pallas_call(
        dct_kernel,
        grid=(steps,),
        in_specs=[
            pl.BlockSpec(block, lambda i: (at, i, 0)),
            pl.BlockSpec(block, lambda i: (at, 2 * steps - 1 - i, 0)),
            pl.BlockSpec(block, lambda i: (at, 2 * steps + i, 0)),
            pl.BlockSpec(block, lambda i: (at, 4 * steps - 1 - i, 0)),
            whole(table.shape),
        ],
        out_specs=[whole(half.shape)] * 2,
        out_shape=[half] * 2,
        scratch_shapes=[
            pltpu.VMEM((4, BAND, STEP), F32),
            pltpu.VMEM((2, STEP, 128), F32),
            pltpu.VMEM((4, BAND, COLS), F32),
        ],
        compiler_params=room(58),
        cost_estimate=pl.CostEstimate(flops=3_500_000_000, bytes_accessed=6_000_000, transcendentals=0),
        name="dct",
    )(*([snapshots] * 4), table)


def place_of_own():
    return tuple(lax.axis_index(name) for name in ("z", "x", "c", "y"))


def own_weights(snap, z, x, core):
    chip = (z * NX + x) * 4
    return [snap[pl.ds(chip + 2 * owner + s, 1), :] for owner in (core, 1 - core) for s in range(2)]


def prepare_kernel(*refs):
    sources, snap, high_t, low_t, weights, blocks = refs[:4], *refs[4:8], refs[8:]
    z, x, core, _ = place_of_own()
    lines = [own_weights(snap, z, lax.rem(x - shift + NX, NX), core) for shift in range(NX)]
    weights[...] = jnp.concatenate(sum(lines, []), axis=0)
    for s in range(4):
        source = sources[s]
        for k in range(4):
            place = slice(HALF * k, HALF * (k + 1))
            high_t[s, :, place], low_t[s, :, place] = split(source[k].T)
            for shift, block in enumerate(blocks):
                start = pl.multiple_of(lax.rem(x + shift, NX) * 32, 32)
                block[s, k] = source[k, pl.ds(start, 32), :]


def prepare(sources, snap):
    crossed = jax.ShapeDtypeStruct((4, COLS, KEEP // 2), BF16)
    block = jax.ShapeDtypeStruct((4, 4, 32, COLS), F32)
    outs = [crossed, crossed, jax.ShapeDtypeStruct((16, RANK), F32)] + [block] * NX
    return pl.pallas_call(
        prepare_kernel,
        in_specs=[VMEM] * 5,
        out_specs=[VMEM] * len(outs),
        out_shape=outs,
        compiler_params=room(12),
        cost_estimate=pl.CostEstimate(flops=10_000_000, bytes_accessed=6_000_000, transcendentals=0),
        name="prepare",
    )(*sources, snap)


def place_rows(x, pieces, rows):
    for shift in range(NX):
        source = lax.rem(x - shift + NX, NX)
        for z in range(NZ):
            start = pl.multiple_of(source * 128 + z * 16, 16)
            for half in range(2):
                rows[half, pl.ds(start, 16), :] = pieces[shift][z, :, 128 * half : 128 * half + 128]


def totals_kernel(high_t, low_t, weights, *refs):
    pieces, (keep, send), (rows, total) = refs[:4], refs[4:6], refs[6:]
    _, x, core, _ = place_of_own()
    place_rows(x, pieces, rows)
    sums = [0.0] * 4
    for k in range(4):
        line = [rows[half, pl.ds(k, HALF, stride=4), :] for half in range(2)]
        lines = split(jnp.concatenate(line, axis=1))
        place = slice(HALF * k, HALF * (k + 1))
        for s in range(4):
            sums[s] += dot3((high_t[s, :, place], low_t[s, :, place]), lines)
    total[...] = sum(part * weights[s : s + 1, :] for s, part in enumerate(sums))
    for shift in range(NX):
        target = lax.rem(x + shift, NX)
        for ref, owner in ((keep, core), (send, 1 - core)):
            start = pl.multiple_of(owner * 128 + target * 32, 32)
            ref[shift] = total[pl.ds(start, 32), :]


def totals(high_t, low_t, weights, pieces):
    part = jax.ShapeDtypeStruct((NX, 32, RANK), F32)
    return pl.pallas_call(
        totals_kernel,
        in_specs=[VMEM] * 7,
        out_specs=[VMEM] * 2,
        out_shape=[part] * 2,
        scratch_shapes=[pltpu.VMEM((2, KEEP // 2, 128), F32), pltpu.VMEM((COLS, RANK), F32)],
        compiler_params=room(12),
        cost_estimate=pl.CostEstimate(flops=800_000_000, bytes_accessed=4_000_000, transcendentals=0),
        name="totals",
    )(high_t, low_t, weights, *pieces)


def row_gram_kernel(*refs):
    pieces, out, rows = refs[:4], refs[4], refs[5]
    place_rows(lax.axis_index("x"), pieces, rows)
    lines = jnp.concatenate([rows[0], rows[1]], axis=1)
    out[...] = exact(lines.T, lines)


def row_gram(pieces):
    return pl.pallas_call(
        row_gram_kernel,
        in_specs=[VMEM] * 4,
        out_specs=VMEM,
        out_shape=jax.ShapeDtypeStruct((RANK, RANK), F32),
        scratch_shapes=[pltpu.VMEM((2, KEEP // 2, 128), F32)],
        compiler_params=room(8),
        cost_estimate=pl.CostEstimate(flops=400_000_000, bytes_accessed=800_000, transcendentals=0),
        name="row_gram",
    )(*pieces)


def inverse(gram, state):
    eye = (
        lax.broadcasted_iota(jnp.int32, (RANK, RANK), 0)
        == lax.broadcasted_iota(jnp.int32, (RANK, RANK), 1)
    ).astype(F32)
    penalty = jnp.sum(gram * eye) / RANK
    system = gram / penalty + eye
    middle = 2.0 / (1.0 + 257.0)
    state[:RANK] = middle * eye
    state[RANK:] = eye - middle * system

    def double(step, reach):
        doubled = 2.0 * reach * reach - 1.0
        gain = 2.0 * reach * reach / doubled
        both = state[...]
        product = gain * dot3(split(both), split(both[RANK:]))
        state[:RANK] = gain * both[:RANK] + product[:RANK]
        state[RANK:] = product[RANK:] - (1.0 / doubled) * eye
        return doubled

    lax.fori_loop(0, 6, double, jnp.float32(258.0 / 256.0))
    found = state[:RANK]
    found = found + dot3(split(found), split(eye - exact(system, found)))
    return found / penalty, penalty


FACTOR, DUAL = RANK + 24, RANK + 24 + COLS


def store_system(found, penalty, weights, inv):
    inv[:RANK] = found
    inv[RANK : RANK + 8] = jnp.full((8, RANK), penalty, F32)
    inv[RANK + 8 : FACTOR] = weights[...]


def col_system_kernel(snap, weights, mine, other, factor, dual, inv, gram, state):
    inv[FACTOR:DUAL] = factor[...]
    inv[DUAL:] = dual[...]
    snaps = snap[...]
    gram[...] = exact(snaps.T, snaps) * (mine[...] + other[...])
    store_system(*inverse(gram[...], state), weights, inv)


def row_system_kernel(snap, weights, mine, other, inv, gram, state):
    core = lax.axis_index("c")
    gram[pl.ds(pl.multiple_of(core * 128, 128), 128), :] = mine[...]
    gram[pl.ds(pl.multiple_of((1 - core) * 128, 128), 128), :] = other[...]
    snaps = snap[...]
    store_system(*inverse(exact(snaps.T, snaps) * gram[...], state), weights, inv)


def system(kernel, rows, *args):
    return pl.pallas_call(
        kernel,
        in_specs=[VMEM] * len(args),
        out_specs=VMEM,
        out_shape=jax.ShapeDtypeStruct((rows, RANK), F32),
        scratch_shapes=[pltpu.VMEM((RANK, RANK), F32), pltpu.VMEM((2 * RANK, RANK), F32)],
        cost_estimate=pl.CostEstimate(flops=3_000_000_000, bytes_accessed=1_000_000, transcendentals=0),
        compiler_params=room(8),
    )(*args)


def admm_update(sums, inv, new, dual_new):
    penalty = inv[RANK, 0]

    def update(step, carry):
        primal, multiplier = new[...], dual_new[...]
        solved = exact(sums[...] + penalty * (primal + multiplier), inv[:RANK])
        primal = jnp.maximum(solved - multiplier, 0.0)
        new[...] = primal
        dual_new[...] = multiplier + primal - solved
        return carry

    lax.fori_loop(0, ADMM_STEPS, update, 0)


def col_kernel(*refs):
    sources, inv, pieces = refs[:4], refs[4], refs[5:13]
    new, dual_new, gram_half, block = refs[13:17]
    total, mapped, gram, held, sems = refs[17:]
    _, x, core, _ = place_of_own()
    copies = [
        pltpu.make_async_copy(source, held.at[at], sems.at[at])
        for at, source in enumerate(sources)
    ]
    for copy in copies:
        copy.start()
    for side in range(NC):
        for shift in range(NX):
            source = lax.rem(x - shift + NX, NX)
            owner = core if side == 0 else 1 - core
            start = pl.multiple_of(owner * 128 + source * 32, 32)
            total[pl.ds(start, 32), :] = pieces[side * NX + shift][...]
    new[...] = inv[FACTOR:DUAL]
    dual_new[...] = inv[DUAL:]
    admm_update(total, inv, new, dual_new)
    primal = new[...]
    gram[...] = exact(primal.T, primal)
    gram_half[...] = gram[pl.ds(pl.multiple_of(core * 128, 128), 128), :]
    lines = split(primal)
    for copy in copies:
        copy.wait()
    gram[:128] = jnp.zeros((128, RANK), F32)

    def add(shift, carry):
        product = dot3(split(held[shift].reshape(512, COLS)), lines)
        for s in range(4):
            weight = inv[pl.ds(RANK + 8 + 4 * shift + s, 1), :]
            gram[:128] += product[128 * s : 128 * s + 128] * weight
        return carry

    lax.fori_loop(0, NX, add, 0)
    sums = gram[:128]
    for k in range(4):
        for half in range(2):
            line = sums[32 * k : 32 * k + 32, 128 * half : 128 * half + 128]
            mapped[half, pl.ds(k, 32, stride=4), :] = line
    for row in range(NZ):
        for half in range(2):
            place = slice(128 * half, 128 * half + 128)
            block[row, :, place] = mapped[half, 16 * row : 16 * row + 16, :]


def col_update(coefficients, inv, pieces):
    square = jax.ShapeDtypeStruct((COLS, RANK), F32)
    block = jax.ShapeDtypeStruct((NZ, 16, RANK), F32)
    outs = [square, square, jax.ShapeDtypeStruct((128, RANK), F32), block]
    return pl.pallas_call(
        col_kernel,
        in_specs=[pl.BlockSpec(memory_space=pltpu.HBM)] * 4 + [VMEM] * 9,
        out_specs=[VMEM] * len(outs),
        out_shape=outs,
        scratch_shapes=[
            pltpu.VMEM((COLS, RANK), F32),
            pltpu.VMEM((2, 128, 128), F32),
            pltpu.VMEM((RANK, RANK), F32),
            pltpu.VMEM((NX, 4, 4, 32, COLS), F32),
            pltpu.SemaphoreType.DMA((4,)),
        ],
        cost_estimate=pl.CostEstimate(flops=1_500_000_000, bytes_accessed=5_000_000, transcendentals=0),
        compiler_params=room(16),
        name="col_update",
    )(*coefficients, inv, *pieces)


def gram_sum_kernel(*refs):
    parts, out, held = refs[:4], refs[4], refs[5]
    y = lax.axis_index("y")
    for shift in range(NY):
        held[lax.rem(y - shift + NY, NY)] = parts[shift][...]
    out[...] = (held[0] + held[1]) + (held[2] + held[3])


def gram_sum(parts):
    shape = parts[0].shape
    return pl.pallas_call(
        gram_sum_kernel,
        in_specs=[VMEM] * NY,
        out_specs=VMEM,
        out_shape=jax.ShapeDtypeStruct(shape, F32),
        scratch_shapes=[pltpu.VMEM((NY, *shape), F32)],
        compiler_params=room(4),
        name="gram_sum",
    )(*parts)


def row_kernel(inv, factor, dual, mine, other, new, dual_new, sums):
    sums[...] = mine[...] + other[...]
    new[...] = factor[...]
    dual_new[...] = dual[...]
    admm_update(sums, inv, new, dual_new)


def row_update(inv, factor, dual, mine, other):
    own = jax.ShapeDtypeStruct((16, RANK), F32)
    return pl.pallas_call(
        row_kernel,
        in_specs=[VMEM] * 5,
        out_specs=[VMEM] * 2,
        out_shape=[own] * 2,
        scratch_shapes=[pltpu.VMEM((16, RANK), F32)],
        compiler_params=room(4),
        name="row_update",
    )(inv, factor, dual, mine, other)


def shifted(array, axis, size, by):
    return lax.ppermute(array, axis, [(i, (i + by) % size) for i in range(size)])


def swapped(array, axis, flip):
    return lax.ppermute(array, axis, [(i, i ^ flip) for i in range(4)])


def sum_kernel(count, *refs):
    total = refs[0][...]
    for ref in refs[1:count]:
        total = total + ref[...]
    outs = refs[count:]
    for at, out in enumerate(outs):
        share = total.shape[0] // len(outs)
        own = total if len(outs) == 1 else total[at * share : (at + 1) * share]
        out[...] = own.reshape(out.shape)


def summed(parts, shape, count=1):
    return pl.pallas_call(
        functools.partial(sum_kernel, len(parts)),
        in_specs=[VMEM] * len(parts),
        out_specs=[VMEM] * count,
        out_shape=[jax.ShapeDtypeStruct(shape, F32)] * count,
        compiler_params=room(8),
        name="summed",
    )(*parts)


def spread_kernel(count, *refs):
    total = refs[0][...]
    for ref in refs[1:count]:
        total = total + ref[...]
    for at in range(refs[count].shape[0]):
        refs[count][at] = total


def copied_along(parts, axes, size):
    whole = pl.pallas_call(
        functools.partial(spread_kernel, len(parts)),
        in_specs=[VMEM] * len(parts),
        out_specs=VMEM,
        out_shape=jax.ShapeDtypeStruct((size, *parts[0].shape), F32),
        compiler_params=room(8),
        name="spread",
    )(*parts)
    return lax.all_to_all(whole, axes, 0, 0, tiled=True)


def fold_kernel(block, out):
    half = [block[at] + block[at + 1] for at in range(0, NZ, 2)]
    out[...] = (half[0] + half[1]) + (half[2] + half[3])


def folded(block):
    return pl.pallas_call(
        fold_kernel,
        in_specs=[VMEM],
        out_specs=VMEM,
        out_shape=jax.ShapeDtypeStruct(block.shape[1:], F32),
        compiler_params=room(4),
        name="folded",
    )(block)


def around(array, axis):
    moved = []
    for by in range(1, 4):
        given = array[by] if isinstance(array, list) else array
        moved.append(shifted(given, axis, 4, by))
    return moved


def update(snapshots, snap_factor, row_factor, col_factor, row_dual, col_dual):
    mine = copied_along([row_factor], "z", NZ)
    table = twiddles()
    early, send_early = dct(snapshots, table, 0)
    mine, early, send_early = lax.optimization_barrier((mine, early, send_early))
    lines = [mine, *around(mine, "x")]
    late, send_late = dct(snapshots, table, 1)
    others = [shifted(send, "c", NC, 1) for send in (send_early, send_late)]
    high_t, low_t, weights, *blocks = prepare([early, late, *others], snap_factor)
    keep, send = totals(high_t, low_t, weights, lines)
    gram = row_gram(lines)
    other = shifted(gram, "c", NC, 1)
    args = snap_factor, weights, gram, other
    inv = system(col_system_kernel, DUAL + COLS, *args, col_factor, col_dual)
    parts = list(summed([keep, shifted(send, "c", NC, 1)], (32, RANK), NX))
    chunk = copied_along([parts[0], *around(parts, "x")], "z", NZ)
    coefficients = [blocks[0], *around(list(blocks), "x")]
    chunk, inv = lax.optimization_barrier((chunk, inv))
    chunk = folded(chunk)
    pieces = [chunk, *around(chunk, "x")]
    pieces = pieces + [shifted(piece, "c", NC, 1) for piece in pieces]
    col_new, col_dual_new, gram_half, block = col_update(coefficients, inv, pieces)
    grams = [gram_half, *around(gram_half, "y")]
    gram_mine = gram_sum(grams)
    other = shifted(gram_mine, "c", NC, 1)
    args = snap_factor, weights, gram_mine, other
    inv = system(row_system_kernel, FACTOR, *args)
    block = lax.all_to_all(block, "z", 0, 0, tiled=True)
    mine = folded(block)
    near = swapped(mine, "y", 1)
    near = summed([mine, near], mine.shape)[0]
    far = swapped(near, "y", 3)
    row_new, row_dual_new = row_update(inv, row_factor, row_dual, near, far)
    return row_new, col_new, row_dual_new, col_dual_new


def solution(mesh):
    fine = Mesh(mesh.devices.reshape(NZ, NX, NC, NY), ("z", "x", "c", "y"))
    return jax.shard_map(
        update,
        mesh=fine,
        in_specs=(
            P(WIDE, None, "y"),
            P(),
            P(WIDE, None),
            P("y", None),
            P(WIDE, None),
            P("y", None),
        ),
        out_specs=(P(WIDE, None), P("y", None), P(WIDE, None), P("y", None)),
        check_vma=False,
    )
```

```python
import functools
import math

import jax
import jax.numpy as jnp
import numpy as np
from jax import lax
from jax.experimental import pallas as pl
from jax.experimental.pallas import tpu as pltpu
from jax.sharding import Mesh
from jax.sharding import PartitionSpec as P


ROWS = 4096
KEEP = 1024
RANK = 256
COLS = 256
ADMM_STEPS = 3
PART = ROWS // 4
BAND = KEEP // 4
HALF = BAND // 2
STEP = 256
NZ, NX, NC, NY = 8, 4, 2, 4
WIDE = ("z", "x", "c")
F32 = jnp.float32
BF16 = jnp.bfloat16
VMEM = pl.BlockSpec(memory_space=pltpu.VMEM)


def twiddles():
    odd = 2 * np.arange(STEP)[None, :] + 1
    sizes = (NC, NX, NZ, 4)
    half, x, z, low = np.meshgrid(*map(np.arange, sizes), indexing="ij")
    degree = (8 * (NX * z + x) + 4 * half + low).reshape(BAND, 1)
    scale = math.sqrt(2.0 / ROWS)
    angles = np.pi * odd * degree / 2048, np.pi * odd * (2 * degree + 1) / 4096
    weight = np.where(degree == 0, math.sqrt(1.0 / ROWS), scale), scale
    base = [w * f(a) for w, a in zip(weight, angles) for f in (np.cos, np.sin)]
    lanes = np.ones((1, 128))
    eight = np.arange(8)[:, None] * lanes
    near = np.stack([np.arange(8)[:, None] % 4 * lanes, np.arange(8)[:, None] % 4 * lanes + 4])
    ahead = [f(a) for a in (np.pi * near / 4, np.pi * (2 * near + 1) / 8) for f in (np.cos, np.sin)]
    turn = np.pi * (2 * eight + 1) / 8192
    turns = [np.cos(turn), np.sin(turn)] * 2
    parts = [base, [np.concatenate(part) for part in ahead], turns]
    parts = [np.stack([np.tile(p, (1, STEP // p.shape[1])) for p in part]) for part in parts]
    return jnp.asarray(np.concatenate(parts, axis=1).astype(np.float32))


def room(mebibytes):
    return pltpu.CompilerParams(vmem_limit_bytes=mebibytes * 2**20)


def split(value):
    high = value.astype(BF16)
    return high, (value - high.astype(F32)).astype(BF16)


def dot(a, b):
    return jnp.dot(a, b, preferred_element_type=F32)


def dot3(a, b):
    return dot(a[0], b[0]) + (dot(a[1], b[0]) + dot(a[0], b[1]))


def exact(a, b):
    return jnp.dot(a, b, precision=lax.Precision.HIGHEST, preferred_element_type=F32)


def twice(value):
    return jnp.concatenate([value, value], axis=1)


def turned(ref, s):
    index = 7 - lax.broadcasted_iota(jnp.int32, (8, COLS), 0)
    tiles = []
    for t in range(STEP // 8):
        tile = ref[s, STEP - 8 * (t + 1) : STEP - 8 * t, :]
        tiles.append(jnp.take_along_axis(tile, index, axis=0, mode="promise_in_bounds"))
    return jnp.concatenate(tiles, axis=0)


def dct_kernel(x0, x1, x2, x3, table, keep, send, held, rotated, total):
    step = pl.program_id(0)

    @pl.when(step == 0)
    def _():
        total[...] = jnp.zeros_like(total)
        held[...] = table[:, :BAND]
        cos, sin = table[0, BAND + 16 :, :128], table[1, BAND + 16 :, :128]
        for t in range(STEP // 8):
            by_cos, by_sin = math.cos(math.pi * t / 512), math.sin(math.pi * t / 512)
            rotated[0, 8 * t : 8 * t + 8, :] = cos * by_cos - sin * by_sin
            rotated[1, 8 * t : 8 * t + 8, :] = sin * by_cos + cos * by_sin

    @pl.when(step > 0)
    def _():
        for pair in range(2):
            cos, sin = held[2 * pair], held[2 * pair + 1]
            by_cos, by_sin = (
                jnp.concatenate(
                    [table[at, BAND : BAND + 8]] * 16 + [table[at, BAND + 8 : BAND + 16]] * 16, axis=0
                )
                for at in (2 * pair, 2 * pair + 1)
            )
            held[2 * pair] = cos * by_cos - sin * by_sin
            held[2 * pair + 1] = sin * by_cos + cos * by_sin
        cos, sin = rotated[0], rotated[1]
        by_cos, by_sin = math.cos(math.pi / 16), math.sin(math.pi / 16)
        rotated[0] = cos * by_cos - sin * by_sin
        rotated[1] = sin * by_cos + cos * by_sin

    plain, even, odd = split(held[0]), split(held[2]), split(held[3])
    cos, sin = twice(rotated[0]), twice(rotated[1])
    for s in range(2):
        first, third = x0[s], x2[s]
        second, fourth = turned(x1, s), turned(x3, s)
        outer, inner = first + fourth, second + third
        v, w = first - fourth, second - third
        total[s, 0] += dot3(plain, split(outer + inner))
        total[s, 2] += dot3(even, split(outer - inner))
        p = dot3(even, split(v * cos - w * sin))
        q = dot3(odd, split(v * sin + w * cos))
        total[s, 1] += p + q
        total[s, 3] += p - q

    @pl.when(step == pl.num_programs(0) - 1)
    def _():
        core = lax.axis_index("c")
        for ref, owner in ((keep, core), (send, 1 - core)):
            for s in range(2):
                for k in range(4):
                    ref[s, k] = total[s, k, pl.ds(pl.multiple_of(owner * HALF, HALF), HALF), :]


def dct(snapshots, table):
    steps = PART // STEP
    block = (2, STEP, COLS)
    half = jax.ShapeDtypeStruct((2, 4, HALF, COLS), F32)

    def whole(shape):
        return pl.BlockSpec(shape, lambda i: (0,) * len(shape))

    return pl.pallas_call(
        dct_kernel,
        grid=(steps,),
        in_specs=[
            pl.BlockSpec(block, lambda i: (0, i, 0)),
            pl.BlockSpec(block, lambda i: (0, 2 * steps - 1 - i, 0)),
            pl.BlockSpec(block, lambda i: (0, 2 * steps + i, 0)),
            pl.BlockSpec(block, lambda i: (0, 4 * steps - 1 - i, 0)),
            whole(table.shape),
        ],
        out_specs=[whole(half.shape)] * 2,
        out_shape=[half] * 2,
        scratch_shapes=[
            pltpu.VMEM((4, BAND, STEP), F32),
            pltpu.VMEM((2, STEP, 128), F32),
            pltpu.VMEM((2, 4, BAND, COLS), F32),
        ],
        compiler_params=room(58),
        cost_estimate=pl.CostEstimate(flops=7_000_000_000, bytes_accessed=12_000_000, transcendentals=0),
        name="dct",
    )(*([snapshots] * 4), table)


def place_of_own():
    return tuple(lax.axis_index(name) for name in ("z", "x", "c", "y"))


def own_weights(snap, z, x, core):
    chip = (z * NX + x) * 4
    return [snap[pl.ds(chip + 2 * owner + s, 1), :] for owner in (core, 1 - core) for s in range(2)]


def prepare_kernel(*refs):
    own, other, snap, high_t, low_t, weights = refs[:6]
    blocks = refs[6:]
    z, x, core, _ = place_of_own()
    lines = [own_weights(snap, z, lax.rem(x - shift + NX, NX), core) for shift in range(NX)]
    weights[...] = jnp.concatenate(sum(lines, []), axis=0)
    for s in range(4):
        source = own if s < 2 else other
        for k in range(4):
            place = slice(HALF * k, HALF * (k + 1))
            high_t[s, :, place], low_t[s, :, place] = split(source[s % 2, k].T)
            for shift, block in enumerate(blocks):
                start = pl.multiple_of(lax.rem(x + shift, NX) * 32, 32)
                block[s, k] = source[s % 2, k, pl.ds(start, 32), :]


def prepare(own, other, snap):
    crossed = jax.ShapeDtypeStruct((4, COLS, KEEP // 2), BF16)
    block = jax.ShapeDtypeStruct((4, 4, 32, COLS), F32)
    outs = [crossed, crossed, jax.ShapeDtypeStruct((16, RANK), F32)] + [block] * NX
    return pl.pallas_call(
        prepare_kernel,
        in_specs=[VMEM] * 3,
        out_specs=[VMEM] * len(outs),
        out_shape=outs,
        compiler_params=room(12),
        cost_estimate=pl.CostEstimate(flops=10_000_000, bytes_accessed=6_000_000, transcendentals=0),
        name="prepare",
    )(own, other, snap)


def place_rows(x, pieces, rows):
    for shift in range(NX):
        source = lax.rem(x - shift + NX, NX)
        for z in range(NZ):
            start = pl.multiple_of(source * 128 + z * 16, 16)
            for half in range(2):
                rows[half, pl.ds(start, 16), :] = pieces[shift][z, :, 128 * half : 128 * half + 128]


def totals_kernel(high_t, low_t, weights, *refs):
    pieces, (keep, send), (rows, total) = refs[:4], refs[4:6], refs[6:]
    _, x, core, _ = place_of_own()
    place_rows(x, pieces, rows)
    sums = [0.0] * 4
    for k in range(4):
        line = [rows[half, pl.ds(k, HALF, stride=4), :] for half in range(2)]
        lines = split(jnp.concatenate(line, axis=1))
        place = slice(HALF * k, HALF * (k + 1))
        for s in range(4):
            sums[s] += dot3((high_t[s, :, place], low_t[s, :, place]), lines)
    total[...] = sum(part * weights[s : s + 1, :] for s, part in enumerate(sums))
    for shift in range(NX):
        target = lax.rem(x + shift, NX)
        for ref, owner in ((keep, core), (send, 1 - core)):
            start = pl.multiple_of(owner * 128 + target * 32, 32)
            ref[shift] = total[pl.ds(start, 32), :]


def totals(high_t, low_t, weights, pieces):
    part = jax.ShapeDtypeStruct((NX, 32, RANK), F32)
    return pl.pallas_call(
        totals_kernel,
        in_specs=[VMEM] * 7,
        out_specs=[VMEM] * 2,
        out_shape=[part] * 2,
        scratch_shapes=[pltpu.VMEM((2, KEEP // 2, 128), F32), pltpu.VMEM((COLS, RANK), F32)],
        compiler_params=room(12),
        cost_estimate=pl.CostEstimate(flops=800_000_000, bytes_accessed=4_000_000, transcendentals=0),
        name="totals",
    )(high_t, low_t, weights, *pieces)


def row_gram_kernel(*refs):
    pieces, out, rows = refs[:4], refs[4], refs[5]
    place_rows(lax.axis_index("x"), pieces, rows)
    lines = jnp.concatenate([rows[0], rows[1]], axis=1)
    out[...] = exact(lines.T, lines)


def row_gram(pieces):
    return pl.pallas_call(
        row_gram_kernel,
        in_specs=[VMEM] * 4,
        out_specs=VMEM,
        out_shape=jax.ShapeDtypeStruct((RANK, RANK), F32),
        scratch_shapes=[pltpu.VMEM((2, KEEP // 2, 128), F32)],
        compiler_params=room(8),
        cost_estimate=pl.CostEstimate(flops=400_000_000, bytes_accessed=800_000, transcendentals=0),
        name="row_gram",
    )(*pieces)


def inverse(gram, state):
    eye = (
        lax.broadcasted_iota(jnp.int32, (RANK, RANK), 0)
        == lax.broadcasted_iota(jnp.int32, (RANK, RANK), 1)
    ).astype(F32)
    penalty = jnp.sum(gram * eye) / RANK
    system = gram / penalty + eye
    middle = 2.0 / (1.0 + 257.0)
    state[:RANK] = middle * eye
    state[RANK:] = eye - middle * system

    def double(step, reach):
        doubled = 2.0 * reach * reach - 1.0
        gain = 2.0 * reach * reach / doubled
        both = state[...]
        product = gain * dot3(split(both), split(both[RANK:]))
        state[:RANK] = gain * both[:RANK] + product[:RANK]
        state[RANK:] = product[RANK:] - (1.0 / doubled) * eye
        return doubled

    lax.fori_loop(0, 6, double, jnp.float32(258.0 / 256.0))
    found = state[:RANK]
    found = found + dot3(split(found), split(eye - exact(system, found)))
    return found / penalty, penalty


FACTOR, DUAL = RANK + 24, RANK + 24 + COLS


def store_system(found, penalty, weights, inv):
    inv[:RANK] = found
    inv[RANK : RANK + 8] = jnp.full((8, RANK), penalty, F32)
    inv[RANK + 8 : FACTOR] = weights[...]


def col_system_kernel(snap, weights, mine, other, factor, dual, inv, gram, state):
    inv[FACTOR:DUAL] = factor[...]
    inv[DUAL:] = dual[...]
    snaps = snap[...]
    gram[...] = exact(snaps.T, snaps) * (mine[...] + other[...])
    store_system(*inverse(gram[...], state), weights, inv)


def row_system_kernel(snap, weights, mine, other, inv, gram, state):
    core = lax.axis_index("c")
    gram[pl.ds(pl.multiple_of(core * 128, 128), 128), :] = mine[...]
    gram[pl.ds(pl.multiple_of((1 - core) * 128, 128), 128), :] = other[...]
    snaps = snap[...]
    store_system(*inverse(exact(snaps.T, snaps) * gram[...], state), weights, inv)


def system(kernel, rows, *args):
    return pl.pallas_call(
        kernel,
        in_specs=[VMEM] * len(args),
        out_specs=VMEM,
        out_shape=jax.ShapeDtypeStruct((rows, RANK), F32),
        scratch_shapes=[pltpu.VMEM((RANK, RANK), F32), pltpu.VMEM((2 * RANK, RANK), F32)],
        cost_estimate=pl.CostEstimate(flops=3_000_000_000, bytes_accessed=1_000_000, transcendentals=0),
        compiler_params=room(8),
    )(*args)


def admm_update(sums, inv, new, dual_new):
    penalty = inv[RANK, 0]

    def update(step, carry):
        primal, multiplier = new[...], dual_new[...]
        solved = exact(sums[...] + penalty * (primal + multiplier), inv[:RANK])
        primal = jnp.maximum(solved - multiplier, 0.0)
        new[...] = primal
        dual_new[...] = multiplier + primal - solved
        return carry

    lax.fori_loop(0, ADMM_STEPS, update, 0)


def col_kernel(*refs):
    sources, inv, pieces = refs[:4], refs[4], refs[5:13]
    new, dual_new, gram_half, block = refs[13:17]
    total, mapped, gram, held, sems = refs[17:]
    _, x, core, _ = place_of_own()
    copies = [
        pltpu.make_async_copy(source, held.at[at], sems.at[at])
        for at, source in enumerate(sources)
    ]
    for copy in copies:
        copy.start()
    for side in range(NC):
        for shift in range(NX):
            source = lax.rem(x - shift + NX, NX)
            owner = core if side == 0 else 1 - core
            start = pl.multiple_of(owner * 128 + source * 32, 32)
            total[pl.ds(start, 32), :] = pieces[side * NX + shift][...]
    new[...] = inv[FACTOR:DUAL]
    dual_new[...] = inv[DUAL:]
    admm_update(total, inv, new, dual_new)
    primal = new[...]
    gram[...] = exact(primal.T, primal)
    gram_half[...] = gram[pl.ds(pl.multiple_of(core * 128, 128), 128), :]
    lines = split(primal)
    for copy in copies:
        copy.wait()
    gram[:128] = jnp.zeros((128, RANK), F32)

    def add(shift, carry):
        product = dot3(split(held[shift].reshape(512, COLS)), lines)
        for s in range(4):
            weight = inv[pl.ds(RANK + 8 + 4 * shift + s, 1), :]
            gram[:128] += product[128 * s : 128 * s + 128] * weight
        return carry

    lax.fori_loop(0, NX, add, 0)
    sums = gram[:128]
    for k in range(4):
        for half in range(2):
            line = sums[32 * k : 32 * k + 32, 128 * half : 128 * half + 128]
            mapped[half, pl.ds(k, 32, stride=4), :] = line
    for row in range(NZ):
        for half in range(2):
            place = slice(128 * half, 128 * half + 128)
            block[row, :, place] = mapped[half, 16 * row : 16 * row + 16, :]


def col_update(coefficients, inv, pieces):
    square = jax.ShapeDtypeStruct((COLS, RANK), F32)
    block = jax.ShapeDtypeStruct((NZ, 16, RANK), F32)
    outs = [square, square, jax.ShapeDtypeStruct((128, RANK), F32), block]
    return pl.pallas_call(
        col_kernel,
        in_specs=[pl.BlockSpec(memory_space=pltpu.HBM)] * 4 + [VMEM] * 9,
        out_specs=[VMEM] * len(outs),
        out_shape=outs,
        scratch_shapes=[
            pltpu.VMEM((COLS, RANK), F32),
            pltpu.VMEM((2, 128, 128), F32),
            pltpu.VMEM((RANK, RANK), F32),
            pltpu.VMEM((NX, 4, 4, 32, COLS), F32),
            pltpu.SemaphoreType.DMA((4,)),
        ],
        cost_estimate=pl.CostEstimate(flops=1_500_000_000, bytes_accessed=5_000_000, transcendentals=0),
        compiler_params=room(16),
        name="col_update",
    )(*coefficients, inv, *pieces)


def row_kernel(inv, factor, dual, mine, other, new, dual_new, sums):
    sums[...] = mine[...] + other[...]
    new[...] = factor[...]
    dual_new[...] = dual[...]
    admm_update(sums, inv, new, dual_new)


def row_update(inv, factor, dual, mine, other):
    own = jax.ShapeDtypeStruct((16, RANK), F32)
    return pl.pallas_call(
        row_kernel,
        in_specs=[VMEM] * 5,
        out_specs=[VMEM] * 2,
        out_shape=[own] * 2,
        scratch_shapes=[pltpu.VMEM((16, RANK), F32)],
        compiler_params=room(4),
        name="row_update",
    )(inv, factor, dual, mine, other)


def shifted(array, axis, size, by):
    return lax.ppermute(array, axis, [(i, (i + by) % size) for i in range(size)])


def swapped(array, axis, flip):
    return lax.ppermute(array, axis, [(i, i ^ flip) for i in range(4)])


def sum_kernel(count, *refs):
    total = refs[0][...]
    for ref in refs[1:count]:
        total = total + ref[...]
    outs = refs[count:]
    for at, out in enumerate(outs):
        share = total.shape[0] // len(outs)
        own = total if len(outs) == 1 else total[at * share : (at + 1) * share]
        out[...] = own.reshape(out.shape)


def summed(parts, shape, count=1):
    return pl.pallas_call(
        functools.partial(sum_kernel, len(parts)),
        in_specs=[VMEM] * len(parts),
        out_specs=[VMEM] * count,
        out_shape=[jax.ShapeDtypeStruct(shape, F32)] * count,
        compiler_params=room(8),
        name="summed",
    )(*parts)


def spread_kernel(count, *refs):
    total = refs[0][...]
    for ref in refs[1:count]:
        total = total + ref[...]
    for at in range(refs[count].shape[0]):
        refs[count][at] = total


def copied_along(parts, axes, size):
    whole = pl.pallas_call(
        functools.partial(spread_kernel, len(parts)),
        in_specs=[VMEM] * len(parts),
        out_specs=VMEM,
        out_shape=jax.ShapeDtypeStruct((size, *parts[0].shape), F32),
        compiler_params=room(8),
        name="spread",
    )(*parts)
    return lax.all_to_all(whole, axes, 0, 0, tiled=True)


def fold_kernel(block, out):
    half = [block[at] + block[at + 1] for at in range(0, NZ, 2)]
    out[...] = (half[0] + half[1]) + (half[2] + half[3])


def folded(block):
    return pl.pallas_call(
        fold_kernel,
        in_specs=[VMEM],
        out_specs=VMEM,
        out_shape=jax.ShapeDtypeStruct(block.shape[1:], F32),
        compiler_params=room(4),
        name="folded",
    )(block)


def around(array, axis):
    moved = []
    for by in range(1, 4):
        given = array[by] if isinstance(array, list) else array
        moved.append(shifted(given, axis, 4, by))
    return moved


def update(snapshots, snap_factor, row_factor, col_factor, row_dual, col_dual):
    mine = copied_along([row_factor], "z", NZ)
    own, send = dct(snapshots, twiddles())
    mine, own, send = lax.optimization_barrier((mine, own, send))
    lines = [mine, *around(mine, "x")]
    high_t, low_t, weights, *blocks = prepare(own, shifted(send, "c", NC, 1), snap_factor)
    keep, send = totals(high_t, low_t, weights, lines)
    gram = row_gram(lines)
    other = shifted(gram, "c", NC, 1)
    args = snap_factor, weights, gram, other
    inv = system(col_system_kernel, DUAL + COLS, *args, col_factor, col_dual)
    parts = list(summed([keep, shifted(send, "c", NC, 1)], (32, RANK), NX))
    parts = [parts[0], *around(parts, "x")]
    chunk = copied_along(parts, "z", NZ)
    coefficients = [blocks[0], *around(list(blocks), "x")]
    chunk, inv = lax.optimization_barrier((chunk, inv))
    chunk = folded(chunk)
    pieces = [chunk, *around(chunk, "x")]
    pieces = pieces + [shifted(piece, "c", NC, 1) for piece in pieces]
    col_new, col_dual_new, gram_half, block = col_update(coefficients, inv, pieces)
    other = swapped(gram_half, "y", 1)
    gram_near = summed([gram_half, other], gram_half.shape)[0]
    other = swapped(gram_near, "y", 3)
    gram_mine = summed([gram_near, other], gram_half.shape)[0]
    other = shifted(gram_mine, "c", NC, 1)
    args = snap_factor, weights, gram_mine, other
    inv = system(row_system_kernel, FACTOR, *args)
    block = lax.all_to_all(block, "z", 0, 0, tiled=True)
    mine = folded(block)
    near = swapped(mine, "y", 1)
    near = summed([mine, near], mine.shape)[0]
    far = swapped(near, "y", 3)
    row_new, row_dual_new = row_update(inv, row_factor, row_dual, near, far)
    return row_new, col_new, row_dual_new, col_dual_new


def solution(mesh):
    fine = Mesh(mesh.devices.reshape(NZ, NX, NC, NY), ("z", "x", "c", "y"))
    return jax.shard_map(
        update,
        mesh=fine,
        in_specs=(
            P(WIDE, None, "y"),
            P(),
            P(WIDE, None),
            P("y", None),
            P(WIDE, None),
            P("y", None),
        ),
        out_specs=(P(WIDE, None), P("y", None), P(WIDE, None), P("y", None)),
        check_vma=False,
    )
```

```python
import functools
import math

import jax
import jax.numpy as jnp
import numpy as np
from jax import lax
from jax.experimental import pallas as pl
from jax.experimental.pallas import tpu as pltpu
from jax.sharding import Mesh
from jax.sharding import PartitionSpec as P


ROWS = 4096
KEEP = 1024
RANK = 256
COLS = 256
ADMM_STEPS = 3
PART = ROWS // 4
BAND = KEEP // 4
HALF = BAND // 2
STEP = 256
NZ, NX, NC, NY = 8, 4, 2, 4
WIDE = ("z", "x", "c")
F32 = jnp.float32
BF16 = jnp.bfloat16
VMEM = pl.BlockSpec(memory_space=pltpu.VMEM)


def twiddles():
    odd = 2 * np.arange(STEP)[None, :] + 1
    sizes = (NC, NX, NZ, 4)
    half, x, z, low = np.meshgrid(*map(np.arange, sizes), indexing="ij")
    degree = (8 * (NX * z + x) + 4 * half + low).reshape(BAND, 1)
    scale = math.sqrt(2.0 / ROWS)
    angles = np.pi * odd * degree / 2048, np.pi * odd * (2 * degree + 1) / 4096
    weight = np.where(degree == 0, math.sqrt(1.0 / ROWS), scale), scale
    base = [w * f(a) for w, a in zip(weight, angles) for f in (np.cos, np.sin)]
    lanes = np.ones((1, 128))
    eight = np.arange(8)[:, None] * lanes
    near = np.stack([np.arange(8)[:, None] % 4 * lanes, np.arange(8)[:, None] % 4 * lanes + 4])
    ahead = [f(a) for a in (np.pi * near / 4, np.pi * (2 * near + 1) / 8) for f in (np.cos, np.sin)]
    turn = np.pi * (2 * eight + 1) / 8192
    turns = [np.cos(turn), np.sin(turn)] * 2
    parts = [base, [np.concatenate(part) for part in ahead], turns]
    parts = [np.stack([np.tile(p, (1, STEP // p.shape[1])) for p in part]) for part in parts]
    return jnp.asarray(np.concatenate(parts, axis=1).astype(np.float32))


def room(mebibytes):
    return pltpu.CompilerParams(vmem_limit_bytes=mebibytes * 2**20)


def split(value):
    high = value.astype(BF16)
    return high, (value - high.astype(F32)).astype(BF16)


def dot(a, b):
    return jnp.dot(a, b, preferred_element_type=F32)


def dot3(a, b):
    return dot(a[0], b[0]) + (dot(a[1], b[0]) + dot(a[0], b[1]))


def exact(a, b):
    return jnp.dot(a, b, precision=lax.Precision.HIGHEST, preferred_element_type=F32)


def twice(value):
    return jnp.concatenate([value, value], axis=1)


def turned(ref, s):
    index = 7 - lax.broadcasted_iota(jnp.int32, (8, COLS), 0)
    tiles = []
    for t in range(STEP // 8):
        tile = ref[s, STEP - 8 * (t + 1) : STEP - 8 * t, :]
        tiles.append(jnp.take_along_axis(tile, index, axis=0, mode="promise_in_bounds"))
    return jnp.concatenate(tiles, axis=0)


def dct_kernel(x0, x1, x2, x3, table, keep, send, held, rotated, total):
    step = pl.program_id(0)

    @pl.when(step == 0)
    def _():
        total[...] = jnp.zeros_like(total)
        held[...] = table[:, :BAND]
        cos, sin = table[0, BAND + 16 :, :128], table[1, BAND + 16 :, :128]
        for t in range(STEP // 8):
            by_cos, by_sin = math.cos(math.pi * t / 512), math.sin(math.pi * t / 512)
            rotated[0, 8 * t : 8 * t + 8, :] = cos * by_cos - sin * by_sin
            rotated[1, 8 * t : 8 * t + 8, :] = sin * by_cos + cos * by_sin

    @pl.when(step > 0)
    def _():
        for pair in range(2):
            cos, sin = held[2 * pair], held[2 * pair + 1]
            by_cos, by_sin = (
                jnp.concatenate(
                    [table[at, BAND : BAND + 8]] * 16 + [table[at, BAND + 8 : BAND + 16]] * 16, axis=0
                )
                for at in (2 * pair, 2 * pair + 1)
            )
            held[2 * pair] = cos * by_cos - sin * by_sin
            held[2 * pair + 1] = sin * by_cos + cos * by_sin
        cos, sin = rotated[0], rotated[1]
        by_cos, by_sin = math.cos(math.pi / 16), math.sin(math.pi / 16)
        rotated[0] = cos * by_cos - sin * by_sin
        rotated[1] = sin * by_cos + cos * by_sin

    plain, even, odd = split(held[0]), split(held[2]), split(held[3])
    cos, sin = twice(rotated[0]), twice(rotated[1])
    for s in range(2):
        first, third = x0[s], x2[s]
        second, fourth = turned(x1, s), turned(x3, s)
        outer, inner = first + fourth, second + third
        v, w = first - fourth, second - third
        total[s, 0] += dot3(plain, split(outer + inner))
        total[s, 2] += dot3(even, split(outer - inner))
        p = dot3(even, split(v * cos - w * sin))
        q = dot3(odd, split(v * sin + w * cos))
        total[s, 1] += p + q
        total[s, 3] += p - q

    @pl.when(step == pl.num_programs(0) - 1)
    def _():
        core = lax.axis_index("c")
        for ref, owner in ((keep, core), (send, 1 - core)):
            for s in range(2):
                for k in range(4):
                    ref[s, k] = total[s, k, pl.ds(pl.multiple_of(owner * HALF, HALF), HALF), :]


def dct(snapshots, table):
    steps = PART // STEP
    block = (2, STEP, COLS)
    half = jax.ShapeDtypeStruct((2, 4, HALF, COLS), F32)

    def whole(shape):
        return pl.BlockSpec(shape, lambda i: (0,) * len(shape))

    return pl.pallas_call(
        dct_kernel,
        grid=(steps,),
        in_specs=[
            pl.BlockSpec(block, lambda i: (0, i, 0)),
            pl.BlockSpec(block, lambda i: (0, 2 * steps - 1 - i, 0)),
            pl.BlockSpec(block, lambda i: (0, 2 * steps + i, 0)),
            pl.BlockSpec(block, lambda i: (0, 4 * steps - 1 - i, 0)),
            whole(table.shape),
        ],
        out_specs=[whole(half.shape)] * 2,
        out_shape=[half] * 2,
        scratch_shapes=[
            pltpu.VMEM((4, BAND, STEP), F32),
            pltpu.VMEM((2, STEP, 128), F32),
            pltpu.VMEM((2, 4, BAND, COLS), F32),
        ],
        compiler_params=room(58),
        cost_estimate=pl.CostEstimate(flops=7_000_000_000, bytes_accessed=12_000_000, transcendentals=0),
        name="dct",
    )(*([snapshots] * 4), table)


def place_of_own():
    return tuple(lax.axis_index(name) for name in ("z", "x", "c", "y"))


def own_weights(snap, z, x, core):
    chip = (z * NX + x) * 4
    return [snap[pl.ds(chip + 2 * owner + s, 1), :] for owner in (core, 1 - core) for s in range(2)]


def prepare_kernel(*refs):
    own, other, snap, high_t, low_t, weights = refs[:6]
    blocks = refs[6:]
    z, x, core, _ = place_of_own()
    lines = [own_weights(snap, z, lax.rem(x - shift + NX, NX), core) for shift in range(NX)]
    weights[...] = jnp.concatenate(sum(lines, []), axis=0)
    for s in range(4):
        source = own if s < 2 else other
        for at in range(NX):
            rows = [source[s % 2, k, 32 * at : 32 * at + 32, :] for k in range(4)]
            place = slice(HALF * at, HALF * at + HALF)
            high_t[s, :, place], low_t[s, :, place] = split(jnp.concatenate(rows, axis=0).T)
        for shift, block in enumerate(blocks):
            start = pl.multiple_of(lax.rem(x + shift, NX) * 32, 32)
            for k in range(4):
                block[s, k] = source[s % 2, k, pl.ds(start, 32), :]


def prepare(own, other, snap):
    crossed = jax.ShapeDtypeStruct((4, COLS, KEEP // 2), BF16)
    block = jax.ShapeDtypeStruct((4, 4, 32, COLS), F32)
    outs = [crossed, crossed, jax.ShapeDtypeStruct((16, RANK), F32)] + [block] * NX
    return pl.pallas_call(
        prepare_kernel,
        in_specs=[VMEM] * 3,
        out_specs=[VMEM] * len(outs),
        out_shape=outs,
        compiler_params=room(12),
        cost_estimate=pl.CostEstimate(flops=10_000_000, bytes_accessed=6_000_000, transcendentals=0),
        name="prepare",
    )(own, other, snap)


def place_rows(x, pieces, rows):
    for shift in range(NX):
        source = lax.rem(x - shift + NX, NX)
        for z in range(NZ):
            start = pl.multiple_of(source * 128 + z * 16, 16)
            for half in range(2):
                rows[half, pl.ds(start, 16), :] = pieces[shift][z, :, 128 * half : 128 * half + 128]


def piece_sums(high_t, low_t, weights, x, shift, piece, rows):
    for z in range(NZ):
        for half in range(2):
            rows[half, 16 * z : 16 * z + 16, :] = piece[z, :, 128 * half : 128 * half + 128]
    lines = [
        jnp.concatenate([rows[half, pl.ds(k, 32, stride=4), :] for half in range(2)], axis=1)
        for k in range(4)
    ]
    lines = split(jnp.concatenate(lines, axis=0))
    start = pl.multiple_of(lax.rem(x - shift + NX, NX) * HALF, HALF)
    total = 0.0
    for s in range(4):
        part = high_t[s, :, pl.ds(start, HALF)], low_t[s, :, pl.ds(start, HALF)]
        total += dot3(part, lines) * weights[s : s + 1, :]
    return total


def early_kernel(high_t, low_t, weights, first, second, third, total, rows):
    x = lax.axis_index("x")
    total[...] = piece_sums(high_t, low_t, weights, x, 0, first, rows)
    total[...] += piece_sums(high_t, low_t, weights, x, 1, second, rows)
    total[...] += piece_sums(high_t, low_t, weights, x, 3, third, rows)


def totals_kernel(high_t, low_t, weights, piece, early, keep, send, rows, total):
    x, core = lax.axis_index("x"), lax.axis_index("c")
    total[...] = early[...] + piece_sums(high_t, low_t, weights, x, 2, piece, rows)
    for shift in range(NX):
        target = lax.rem(x + shift, NX)
        for ref, owner in ((keep, core), (send, 1 - core)):
            start = pl.multiple_of(owner * 128 + target * 32, 32)
            ref[shift] = total[pl.ds(start, 32), :]


def totals(high_t, low_t, weights, pieces):
    rows, total = pltpu.VMEM((2, 128, 128), F32), pltpu.VMEM((COLS, RANK), F32)
    cost = pl.CostEstimate(flops=400_000_000, bytes_accessed=2_000_000, transcendentals=0)
    early = pl.pallas_call(
        early_kernel,
        in_specs=[VMEM] * 6,
        out_specs=VMEM,
        out_shape=jax.ShapeDtypeStruct((COLS, RANK), F32),
        scratch_shapes=[rows],
        compiler_params=room(12),
        cost_estimate=cost,
        name="early_totals",
    )(high_t, low_t, weights, pieces[0], pieces[1], pieces[3])
    part = jax.ShapeDtypeStruct((NX, 32, RANK), F32)
    return pl.pallas_call(
        totals_kernel,
        in_specs=[VMEM] * 5,
        out_specs=[VMEM] * 2,
        out_shape=[part] * 2,
        scratch_shapes=[rows, total],
        compiler_params=room(12),
        cost_estimate=cost,
        name="totals",
    )(high_t, low_t, weights, pieces[2], early)


def row_gram_kernel(*refs):
    pieces, out, rows = refs[:4], refs[4], refs[5]
    place_rows(lax.axis_index("x"), pieces, rows)
    lines = jnp.concatenate([rows[0], rows[1]], axis=1)
    out[...] = exact(lines.T, lines)


def row_gram(pieces):
    return pl.pallas_call(
        row_gram_kernel,
        in_specs=[VMEM] * 4,
        out_specs=VMEM,
        out_shape=jax.ShapeDtypeStruct((RANK, RANK), F32),
        scratch_shapes=[pltpu.VMEM((2, KEEP // 2, 128), F32)],
        compiler_params=room(8),
        cost_estimate=pl.CostEstimate(flops=400_000_000, bytes_accessed=800_000, transcendentals=0),
        name="row_gram",
    )(*pieces)


def inverse(gram, state):
    eye = (
        lax.broadcasted_iota(jnp.int32, (RANK, RANK), 0)
        == lax.broadcasted_iota(jnp.int32, (RANK, RANK), 1)
    ).astype(F32)
    penalty = jnp.sum(gram * eye) / RANK
    system = gram / penalty + eye
    middle = 2.0 / (1.0 + 257.0)
    state[:RANK] = middle * eye
    state[RANK:] = eye - middle * system

    def double(step, reach):
        doubled = 2.0 * reach * reach - 1.0
        gain = 2.0 * reach * reach / doubled
        both = state[...]
        product = gain * dot3(split(both), split(both[RANK:]))
        state[:RANK] = gain * both[:RANK] + product[:RANK]
        state[RANK:] = product[RANK:] - (1.0 / doubled) * eye
        return doubled

    lax.fori_loop(0, 6, double, jnp.float32(258.0 / 256.0))
    found = state[:RANK]
    found = found + dot3(split(found), split(eye - exact(system, found)))
    return found / penalty, penalty


FACTOR, DUAL = RANK + 24, RANK + 24 + COLS


def store_system(found, penalty, weights, inv):
    inv[:RANK] = found
    inv[RANK : RANK + 8] = jnp.full((8, RANK), penalty, F32)
    inv[RANK + 8 : FACTOR] = weights[...]


def col_system_kernel(snap, weights, mine, other, factor, dual, inv, gram, state):
    inv[FACTOR:DUAL] = factor[...]
    inv[DUAL:] = dual[...]
    snaps = snap[...]
    gram[...] = exact(snaps.T, snaps) * (mine[...] + other[...])
    store_system(*inverse(gram[...], state), weights, inv)


def row_system_kernel(snap, weights, mine, other, inv, gram, state):
    core = lax.axis_index("c")
    gram[pl.ds(pl.multiple_of(core * 128, 128), 128), :] = mine[...]
    gram[pl.ds(pl.multiple_of((1 - core) * 128, 128), 128), :] = other[...]
    snaps = snap[...]
    store_system(*inverse(exact(snaps.T, snaps) * gram[...], state), weights, inv)


def system(kernel, rows, *args):
    return pl.pallas_call(
        kernel,
        in_specs=[VMEM] * len(args),
        out_specs=VMEM,
        out_shape=jax.ShapeDtypeStruct((rows, RANK), F32),
        scratch_shapes=[pltpu.VMEM((RANK, RANK), F32), pltpu.VMEM((2 * RANK, RANK), F32)],
        cost_estimate=pl.CostEstimate(flops=3_000_000_000, bytes_accessed=1_000_000, transcendentals=0),
        compiler_params=room(8),
    )(*args)


def admm_update(sums, inv, new, dual_new):
    penalty = inv[RANK, 0]

    def update(step, carry):
        primal, multiplier = new[...], dual_new[...]
        solved = exact(sums[...] + penalty * (primal + multiplier), inv[:RANK])
        primal = jnp.maximum(solved - multiplier, 0.0)
        new[...] = primal
        dual_new[...] = multiplier + primal - solved
        return carry

    lax.fori_loop(0, ADMM_STEPS, update, 0)


def col_kernel(*refs):
    sources, inv, pieces = refs[:4], refs[4], refs[5:13]
    new, dual_new, gram_half, block = refs[13:17]
    total, mapped, gram, held, sems = refs[17:]
    _, x, core, _ = place_of_own()
    copies = [
        pltpu.make_async_copy(source, held.at[at], sems.at[at])
        for at, source in enumerate(sources)
    ]
    for copy in copies:
        copy.start()
    for side in range(NC):
        for shift in range(NX):
            source = lax.rem(x - shift + NX, NX)
            owner = core if side == 0 else 1 - core
            start = pl.multiple_of(owner * 128 + source * 32, 32)
            total[pl.ds(start, 32), :] = pieces[side * NX + shift][...]
    new[...] = inv[FACTOR:DUAL]
    dual_new[...] = inv[DUAL:]
    admm_update(total, inv, new, dual_new)
    primal = new[...]
    gram[...] = exact(primal.T, primal)
    gram_half[...] = gram[pl.ds(pl.multiple_of(core * 128, 128), 128), :]
    lines = split(primal)
    for copy in copies:
        copy.wait()
    gram[:128] = jnp.zeros((128, RANK), F32)

    def add(shift, carry):
        product = dot3(split(held[shift].reshape(512, COLS)), lines)
        for s in range(4):
            weight = inv[pl.ds(RANK + 8 + 4 * shift + s, 1), :]
            gram[:128] += product[128 * s : 128 * s + 128] * weight
        return carry

    lax.fori_loop(0, NX, add, 0)
    sums = gram[:128]
    for k in range(4):
        for half in range(2):
            line = sums[32 * k : 32 * k + 32, 128 * half : 128 * half + 128]
            mapped[half, pl.ds(k, 32, stride=4), :] = line
    for row in range(NZ):
        for half in range(2):
            place = slice(128 * half, 128 * half + 128)
            block[row, :, place] = mapped[half, 16 * row : 16 * row + 16, :]


def col_update(coefficients, inv, pieces):
    square = jax.ShapeDtypeStruct((COLS, RANK), F32)
    block = jax.ShapeDtypeStruct((NZ, 16, RANK), F32)
    outs = [square, square, jax.ShapeDtypeStruct((128, RANK), F32), block]
    return pl.pallas_call(
        col_kernel,
        in_specs=[pl.BlockSpec(memory_space=pltpu.HBM)] * 4 + [VMEM] * 9,
        out_specs=[VMEM] * len(outs),
        out_shape=outs,
        scratch_shapes=[
            pltpu.VMEM((COLS, RANK), F32),
            pltpu.VMEM((2, 128, 128), F32),
            pltpu.VMEM((RANK, RANK), F32),
            pltpu.VMEM((NX, 4, 4, 32, COLS), F32),
            pltpu.SemaphoreType.DMA((4,)),
        ],
        cost_estimate=pl.CostEstimate(flops=1_500_000_000, bytes_accessed=5_000_000, transcendentals=0),
        compiler_params=room(16),
        name="col_update",
    )(*coefficients, inv, *pieces)


def row_kernel(inv, factor, dual, mine, other, new, dual_new, sums):
    sums[...] = mine[...] + other[...]
    new[...] = factor[...]
    dual_new[...] = dual[...]
    admm_update(sums, inv, new, dual_new)


def row_update(inv, factor, dual, mine, other):
    own = jax.ShapeDtypeStruct((16, RANK), F32)
    return pl.pallas_call(
        row_kernel,
        in_specs=[VMEM] * 5,
        out_specs=[VMEM] * 2,
        out_shape=[own] * 2,
        scratch_shapes=[pltpu.VMEM((16, RANK), F32)],
        compiler_params=room(4),
        name="row_update",
    )(inv, factor, dual, mine, other)


def shifted(array, axis, size, by):
    return lax.ppermute(array, axis, [(i, (i + by) % size) for i in range(size)])


def swapped(array, axis, flip):
    return lax.ppermute(array, axis, [(i, i ^ flip) for i in range(4)])


def sum_kernel(count, *refs):
    total = refs[0][...]
    for ref in refs[1:count]:
        total = total + ref[...]
    outs = refs[count:]
    for at, out in enumerate(outs):
        share = total.shape[0] // len(outs)
        own = total if len(outs) == 1 else total[at * share : (at + 1) * share]
        out[...] = own.reshape(out.shape)


def summed(parts, shape, count=1):
    return pl.pallas_call(
        functools.partial(sum_kernel, len(parts)),
        in_specs=[VMEM] * len(parts),
        out_specs=[VMEM] * count,
        out_shape=[jax.ShapeDtypeStruct(shape, F32)] * count,
        compiler_params=room(8),
        name="summed",
    )(*parts)


def spread_kernel(count, *refs):
    total = refs[0][...]
    for ref in refs[1:count]:
        total = total + ref[...]
    for at in range(refs[count].shape[0]):
        refs[count][at] = total


def copied_along(parts, axes, size):
    whole = pl.pallas_call(
        functools.partial(spread_kernel, len(parts)),
        in_specs=[VMEM] * len(parts),
        out_specs=VMEM,
        out_shape=jax.ShapeDtypeStruct((size, *parts[0].shape), F32),
        compiler_params=room(8),
        name="spread",
    )(*parts)
    return lax.all_to_all(whole, axes, 0, 0, tiled=True)


def fold_kernel(block, out):
    half = [block[at] + block[at + 1] for at in range(0, NZ, 2)]
    out[...] = (half[0] + half[1]) + (half[2] + half[3])


def folded(block):
    return pl.pallas_call(
        fold_kernel,
        in_specs=[VMEM],
        out_specs=VMEM,
        out_shape=jax.ShapeDtypeStruct(block.shape[1:], F32),
        compiler_params=room(4),
        name="folded",
    )(block)


def around(array, axis):
    moved = []
    for by in range(1, 4):
        given = array[by] if isinstance(array, list) else array
        moved.append(shifted(given, axis, 4, by))
    return moved


def update(snapshots, snap_factor, row_factor, col_factor, row_dual, col_dual):
    mine = copied_along([row_factor], "z", NZ)
    own, send = dct(snapshots, twiddles())
    mine, own, send = lax.optimization_barrier((mine, own, send))
    lines = [mine, *around(mine, "x")]
    high_t, low_t, weights, *blocks = prepare(own, shifted(send, "c", NC, 1), snap_factor)
    keep, send = totals(high_t, low_t, weights, lines)
    gram = row_gram(lines)
    other = shifted(gram, "c", NC, 1)
    args = snap_factor, weights, gram, other
    inv = system(col_system_kernel, DUAL + COLS, *args, col_factor, col_dual)
    send = shifted(send, "c", NC, 1)
    parts = list(summed([keep, send], (32, RANK), NX))
    parts = [parts[0], *around(parts, "x")]
    chunk = copied_along(parts, "z", NZ)
    coefficients = [blocks[0], *around(list(blocks), "x")]
    chunk, inv = lax.optimization_barrier((chunk, inv))
    chunk = folded(chunk)
    pieces = [chunk, *around(chunk, "x")]
    pieces = pieces + [shifted(piece, "c", NC, 1) for piece in pieces]
    col_new, col_dual_new, gram_half, block = col_update(coefficients, inv, pieces)
    other = swapped(gram_half, "y", 1)
    gram_near = summed([gram_half, other], gram_half.shape)[0]
    other = swapped(gram_near, "y", 3)
    gram_mine = summed([gram_near, other], gram_half.shape)[0]
    other = shifted(gram_mine, "c", NC, 1)
    args = snap_factor, weights, gram_mine, other
    inv = system(row_system_kernel, FACTOR, *args)
    block = lax.all_to_all(block, "z", 0, 0, tiled=True)
    mine = folded(block)
    near = swapped(mine, "y", 1)
    near = summed([mine, near], mine.shape)[0]
    far = swapped(near, "y", 3)
    row_new, row_dual_new = row_update(inv, row_factor, row_dual, near, far)
    return row_new, col_new, row_dual_new, col_dual_new


def solution(mesh):
    fine = Mesh(mesh.devices.reshape(NZ, NX, NC, NY), ("z", "x", "c", "y"))
    return jax.shard_map(
        update,
        mesh=fine,
        in_specs=(
            P(WIDE, None, "y"),
            P(),
            P(WIDE, None),
            P("y", None),
            P(WIDE, None),
            P("y", None),
        ),
        out_specs=(P(WIDE, None), P("y", None), P(WIDE, None), P("y", None)),
        check_vma=False,
    )
```
